32 devices in a mesh: lat: 4 (over z), lon: 8 (over y, x, core).
Axes of the slice: x: 2, y: 2, z: 4, core: 2. Of those that a mesh axis runs over, the one named last changes fastest.
Arguments:
- obs_pert: bfloat16 [2048, 64, 128], P(('lat', 'lon')), may hold values from -6 to 6
- obs_dep: bfloat16 [2048, 64], P(('lat', 'lon')), may hold values from -6 to 6
- obs_prec: bfloat16 [2048, 64], P(('lat', 'lon')), may hold values from 0.25 to 4
- obs_count: int32 [2048], P(('lat', 'lon')), may hold values from 16 to 64
- owner_point: int32 [2048], P(('lat', 'lon')), may hold values from 0 to 2047, as said below
- anomalies: bfloat16 [1, 800, 1600, 128], P(None, 'lat', 'lon'), may hold values from -6 to 6
- flux_mean: float32 [1, 800, 1600], P(None, 'lat', 'lon'), may hold values from -6 to 6
Outputs:
- analysis_anomalies: bfloat16 [1, 800, 1600, 128], P(None, 'lat', 'lon')
- analysis_mean: float32 [1, 800, 1600], P(None, 'lat', 'lon')
The draws below stay inside these ranges and needn't reach their ends.
Inputs may be any that keep to these rules, and one draw needn't show every extreme that they name: owner_point is a permutation of the 2048 coarse point numbers. Of the 64 blocks held by one device, at most 2 belong to points of the tiles of any one device, and exactly 2 for some; every device's tiles get the blocks of all their points.
All inputs are finite; a program needn't handle non-finite values.
Results may differ from the reference program's by a relative error of at most 0.0032.
Values may be sent and summed in bfloat16 or wider, within the bound.
No kernel may reach another device: no remote copies, remote signals or barrier semaphores. Data moves between devices by JAX's collectives and lax.ppermute only.
A program may use at most 256 MiB of HBM per device.

```python
import math
import jax
import jax.numpy as jnp
from jax import lax

K = 128
LAGS = 1
FINE = 25
TILES_LAT = 8
TILES_LON = 8
LOCN = 64
SLOTS = 2048
NPLAT = 32
NPLON = 64
NFLAT = 800
NFLON = 1600
N_LAT = 4
N_LON = 8


def draw_owner_point(key, part):
    devices = N_LAT * N_LON
    holding = TILES_LAT * TILES_LON
    first_key, second_key, third_key = jax.random.split(jax.random.fold_in(key, 11), 3)
    relabel = jax.random.permutation(first_key, devices)
    offset = jax.random.permutation(second_key, devices)
    slot_index = jnp.arange(holding, dtype=jnp.int32)[None, :]
    owners = jnp.arange(devices, dtype=jnp.int32)[:, None]
    home_device = relabel[(offset[owners] + slot_index) % devices]
    shuffles = jax.vmap(lambda sub_key: jax.random.permutation(sub_key, holding))(jax.random.split(third_key, devices))
    within = shuffles[home_device, slot_index]
    point_row = home_device // N_LON * TILES_LAT + within // TILES_LON
    point_col = home_device % N_LON * TILES_LON + within % TILES_LON
    return (point_row * (TILES_LON * N_LON) + point_col).reshape(-1).astype(jnp.int32)


def plant(result, rng, low, largest):
    longest = result.shape.index(max(result.shape))
    spots = []
    for shift in (0, 1):
        where = [jax.random.randint(jax.random.fold_in(rng, axis), (), 0, length) for axis, length in enumerate(result.shape)]
        where[longest] = (where[longest] + shift) % result.shape[longest]
        spots.append(tuple(where))
    return result.at[spots[0]].set(low).at[spots[1]].set(largest)


def level_of(rng, extent, shards, low, high):
    def one(axis_at, blocks):
        steps = jax.random.uniform(jax.random.fold_in(jax.random.fold_in(rng, 6), axis_at), (blocks,), jnp.float32, low / len(shards), high / len(shards))
        return jnp.repeat(jnp.exp(steps), extent[axis_at] // blocks).reshape((-1,) + (1,) * (len(extent) - axis_at - 1))

    loudness = one(*shards[0])
    for cut in shards[1:]:
        loudness = loudness * one(*cut)
    return loudness


def centred(key, dims, scale, bound, cuts=(), kind=jnp.bfloat16):
    entries = scale * jax.random.normal(key, dims, jnp.float32)
    if cuts:
        entries = entries * level_of(key, dims, cuts, -0.22, 0.18)
    return jnp.clip(entries, -bound, bound).astype(kind)


def setup_inputs(seed: int = 0) -> dict:
    key_of = jax.random.split(jax.random.key(seed), 8)
    return {
        "obs_pert": centred(key_of[0], (SLOTS, LOCN, K), 1.0, 6.0, ((0, 32),)),
        "obs_dep": centred(key_of[1], (SLOTS, LOCN), 1.0, 6.0, ((0, 32),)),
        "obs_prec": jnp.clip(jnp.exp(math.log(4.0) - 2.7725887 * jax.random.uniform(key_of[2], (SLOTS, LOCN), jnp.float32) ** level_of(key_of[2], (SLOTS, LOCN), ((0, 32),), -0.2, 0.2)), 0.25, 4.0).astype(jnp.bfloat16),
        "obs_count": plant(jax.random.randint(key_of[3], (SLOTS,), LOCN // 4, LOCN + 1), jax.random.fold_in(key_of[3], 1), LOCN // 4, LOCN).astype(jnp.int32),
        "owner_point": draw_owner_point(jax.random.fold_in(key_of[7], 71), 0),
        "anomalies": centred(key_of[5], (LAGS, NFLAT, NFLON, K), 1.0, 6.0, ((1, 4), (2, 8))),
        "flux_mean": centred(key_of[6], (LAGS, NFLAT, NFLON), 1.0, 6.0, ((1, 4), (2, 8)), jnp.float32),
    }


def solve_blocks(perturbed, departures, weighting):
    members = perturbed.shape[-1]
    values = perturbed.astype(jnp.float32)
    scaled = values * weighting[:, :, None]
    gram_matrix = jnp.einsum('pik,pim->pkm', scaled, values, precision=lax.Precision.HIGHEST)
    right_side = jnp.einsum('pik,pi->pk', scaled, departures.astype(jnp.float32), precision=lax.Precision.HIGHEST)
    identity = jnp.eye(members, dtype=jnp.float32)
    system = gram_matrix + (members - 1.0) * identity
    lower_factor = jnp.linalg.cholesky(system)
    inverse = lax.linalg.triangular_solve(lower_factor, jnp.broadcast_to(identity, system.shape), left_side=True, lower=True)
    transform = (math.sqrt(members - 1.0) * jnp.swapaxes(inverse, 1, 2)).astype(jnp.bfloat16)
    forward = lax.linalg.triangular_solve(lower_factor, right_side[:, :, None], left_side=True, lower=True)
    backward = lax.linalg.triangular_solve(lower_factor, forward, left_side=True, lower=True, transpose_a=True)
    return (transform, backward[:, :, 0].astype(jnp.bfloat16))

def reference(obs_pert, obs_dep, obs_prec, obs_count, owner_point, anomalies, flux_mean):
    devices = N_LAT * N_LON
    holding = TILES_LAT * TILES_LON
    live_slot = jnp.arange(LOCN, dtype=jnp.int32)[None, :] < obs_count[:, None]
    weighting = jnp.where(live_slot, obs_prec.astype(jnp.float32), jnp.zeros((), jnp.float32))

    def solve_group(pieces):
        return solve_blocks(pieces[0], pieces[1], pieces[2])
    transform, mean_weight = lax.map(solve_group, (obs_pert.reshape(devices, holding, LOCN, K), obs_dep.reshape(devices, holding, LOCN), weighting.reshape(devices, holding, LOCN)))
    transform = transform.reshape(devices * holding, K, K)
    mean_weight = mean_weight.reshape(devices * holding, K)
    grid_transform = jnp.zeros((NPLAT * NPLON, K, K), jnp.bfloat16).at[owner_point].set(transform).reshape(NPLAT, NPLON, K, K)
    grid_mean = jnp.zeros((NPLAT * NPLON, K), jnp.bfloat16).at[owner_point].set(mean_weight).reshape(NPLAT, NPLON, K)
    fraction = jnp.arange(FINE, dtype=jnp.float32) / FINE

    def apply_row(index):
        upper_row = jnp.minimum(index + 1, NPLAT - 1)
        lower_t = grid_transform[index]
        upper_t = grid_transform[upper_row]
        lower_m = grid_mean[index]
        upper_m = grid_mean[upper_row]
        fine_rows = lax.dynamic_slice_in_dim(anomalies, index * FINE, FINE, 1).astype(jnp.float32)
        anomaly_field = fine_rows.reshape(LAGS, FINE, NPLON, FINE, K)
        corner_sets = [(lower_t, lower_m, 1.0 - fraction, 1.0 - fraction), (jnp.roll(lower_t, -1, axis=0), jnp.roll(lower_m, -1, axis=0), 1.0 - fraction, fraction), (upper_t, upper_m, fraction, 1.0 - fraction), (jnp.roll(upper_t, -1, axis=0), jnp.roll(upper_m, -1, axis=0), fraction, fraction)]
        summed = jnp.zeros((LAGS, FINE, NPLON, FINE, K), jnp.float32)
        shifted = jnp.zeros((LAGS, FINE, NPLON, FINE), jnp.float32)
        for corner_t, corner_m, lat_weight, lon_weight in corner_sets:
            bilinear = lat_weight[:, None, None] * lon_weight[None, None, :]
            mixed_part = jnp.einsum('libjk,bkm->libjm', anomaly_field, corner_t.astype(jnp.float32))
            summed = summed + bilinear[None, :, :, :, None] * mixed_part
            mean_part = jnp.einsum('libjk,bk->libj', anomaly_field, corner_m.astype(jnp.float32))
            shifted = shifted + bilinear[None] * mean_part
        return (summed.reshape(LAGS, FINE, NFLON, K).astype(jnp.bfloat16), shifted.reshape(LAGS, FINE, NFLON))
    rows_out, means_out = lax.map(apply_row, jnp.arange(NPLAT, dtype=jnp.int32))
    analysis = jnp.transpose(rows_out, (1, 0, 2, 3, 4)).reshape(LAGS, NFLAT, NFLON, K)
    mean_out = flux_mean + jnp.transpose(means_out, (1, 0, 2, 3)).reshape(LAGS, NFLAT, NFLON)
    return (analysis, mean_out)
```

```python
import functools
import math

import jax
import jax.numpy as jnp
from jax import lax
from jax.experimental import pallas as pl
from jax.experimental.pallas import tpu as pltpu
from jax.sharding import PartitionSpec as P

FINE = 25
TILES_LAT = 8
TILES_LON = 8
BLOCK = 16
META = 16
F32 = jnp.float32
BF16 = jnp.bfloat16
NT = (((1,), (1,)), ((), ()))
NN = (((1,), (0,)), ((), ()))


def split(value):
    high = value.astype(BF16)
    return high, (value - high.astype(F32)).astype(BF16)


def dot(left, right, dims=NN):
    return lax.dot_general(left, right, dims, preferred_element_type=F32)


def pack_kernel(columns, lon_devices, capacity, owner, pert, meta, out, ranks):
    slots = out.shape[0]
    holding, locn, _ = pert.shape

    @pl.loop(0, slots // capacity)
    def _(device):
        ranks[device] = 0

    if slots > holding:

        @pl.loop(0, slots)
        def _(slot):
            out[slot, locn:, :] = jnp.full(meta.shape[1:], -1, out.dtype)

    @pl.loop(0, holding)
    def _(block):
        point = owner[block]
        row = point // columns
        col = point % columns
        device = row // TILES_LAT * lon_devices + col // TILES_LON
        rank = ranks[device]
        ranks[device] = rank + 1
        slot = device * capacity + jnp.minimum(rank, capacity - 1)
        out[slot, 0:locn, :] = pert[block]
        out[slot, locn:, :] = meta[block]


def pack(owner, pert, meta, columns, lon_devices, devices, capacity):
    holding, locn, members = pert.shape
    slots = devices * capacity
    return pl.pallas_call(
        functools.partial(pack_kernel, columns, lon_devices, capacity),
        out_shape=jax.ShapeDtypeStruct((slots, locn + META, members), BF16),
        in_specs=[
            pl.BlockSpec(memory_space=pltpu.SMEM),
            pl.BlockSpec(memory_space=pltpu.VMEM),
            pl.BlockSpec(memory_space=pltpu.VMEM),
        ],
        out_specs=pl.BlockSpec(memory_space=pltpu.VMEM),
        scratch_shapes=[pltpu.SMEM((devices,), jnp.int32)],
        name="pack",
    )(owner, pert, meta)


def load_systems(labels, arrived, systems, rights):
    slots, rows, members = arrived.shape
    locn = rows - META
    points = rights.shape[0]
    lane = lax.broadcasted_iota(jnp.int32, (members + META, members), 1)
    eye = lax.broadcasted_iota(jnp.int32, (members, members), 0) == lax.broadcasted_iota(
        jnp.int32, (members, members), 1
    )
    ridge = jnp.where(eye, members - 1.0, 0.0)

    def one(slot):
        label = labels[slot]
        pert = arrived[slot, 0:locn, :]
        meta = arrived[slot, locn:, :].astype(F32)
        weight = meta[0:1]
        depart = meta[1:2]
        twice = jnp.concatenate([pert, pert], axis=0)
        scaled = twice.T.astype(F32) * weight
        line = jnp.broadcast_to(weight * depart, (META, members))
        left = jnp.concatenate([scaled, line], axis=0)
        high = left.astype(BF16).astype(F32)
        both = jnp.where(lane < locn, high, left - high).astype(BF16)
        gram = dot(both, twice)

        def put():
            systems[label] = gram[0:members] + ridge
            rights[pl.ds(label, 1), :] = gram[members : members + 1]

        if slots > points:
            pl.when(label >= 0)(put)
        else:
            put()

    def several(step, carry):
        for part in range(4):
            one(step * 4 + part)
        return carry

    lax.fori_loop(0, slots // 4, several, 0)


def diagonal_inverses(step, systems2d, factors, points, members):
    size = BLOCK
    per = members // size
    lane_block = lax.broadcasted_iota(jnp.int32, (points, members), 1) // size
    rows = []
    for half in range(size // per):
        packed = jnp.zeros((points, members), F32)
        for inner in range(per):
            line = systems2d[pl.ds(size * step + per * half + inner, points, stride=members), :]
            line = pltpu.roll(line, (size * (inner - step)) % members, 1)
            packed = jnp.where(lane_block == inner, line, packed)
        turned = packed.T
        for inner in range(per):
            rows.append(turned[size * inner : size * (inner + 1)])
    sub = lax.broadcasted_iota(jnp.int32, (size, points), 0)
    roots = []
    for k in range(size):
        pivot = jnp.broadcast_to(rows[k][k : k + 1], (size, points))
        root = lax.rsqrt(pivot)
        inverse = root * root
        roots.append(root)
        line = jnp.where(sub == k, 1.0, rows[k])
        scaled = line * inverse
        for i in range(k + 1, size):
            factor = jnp.broadcast_to(rows[i][k : k + 1], (size, points))
            rows[i] = jnp.where(sub == k, 0.0, rows[i]) - factor * scaled
    lower = []
    for i in range(size):
        line = jnp.where(sub < i, rows[i], jnp.where(sub == i, 1.0, 0.0))
        lower.append(line * roots[i])
    whole = []
    for i in range(size):
        total = jnp.zeros((size, points), F32)
        for l in range(i, size):
            total += jnp.broadcast_to(lower[l][i : i + 1], (size, points)) * lower[l]
        whole.append(total)
    for group in range(size // per):
        part = slice(group * per, (group + 1) * per)
        factors[group] = jnp.concatenate(whole[part], axis=0).T
        factors[size // per + group] = jnp.concatenate(lower[part], axis=0).T


def solve_kernel(labels, arrived, own, east, north, corner, systems2d, rights, factors, slabs):
    points = own.shape[0]
    members = own.shape[2]
    systems = systems2d.reshape(points, members, members)
    size = BLOCK
    per = members // size
    groups = 2 * size // per
    load_systems(labels, arrived, systems, rights)
    row8 = lax.broadcasted_iota(jnp.int32, (per, members), 0)
    lane8 = lax.broadcasted_iota(jnp.int32, (per, members), 1)
    own_block = row8 == lane8 // size
    row = lax.broadcasted_iota(jnp.int32, (size, members), 0)
    lane = lax.broadcasted_iota(jnp.int32, (size, members), 1)
    many = 8
    for step in range(members // size):
        diagonal_inverses(step, systems2d, factors, points, members)
        first = step * size
        after = first + size
        here = (lane >= first) & (lane < after)
        unit = jnp.where(lane - first == row, 1.0, 0.0)

        def small(point):
            parts = []
            for group in range(groups):
                line = factors[group, pl.ds(point, 1), :]
                parts.append(jnp.where(own_block, jnp.broadcast_to(line, (per, members)), 0.0))
            left_high, left_low = split(jnp.concatenate(parts, axis=0))
            slab = jnp.where(here, unit, systems[point, first:after, :])
            high, low = split(slab)
            highs = jnp.concatenate([high] * per, axis=0)
            lows = jnp.concatenate([low] * per, axis=0)
            both = dot(
                jnp.concatenate([left_high, left_low], axis=1),
                jnp.concatenate([highs, highs], axis=0),
            ) + dot(left_high, lows)
            systems[point, first:after, :] = jnp.where(lane < after, both[size:], 0.0)
            slabs[point] = both[:size]

        def small_many(index, carry):
            for part in range(many):
                small(index * many + part)
            return carry

        lax.fori_loop(0, points // many, small_many, 0)
        if after == members:
            continue
        rest = members - after
        lane_rest = lax.broadcasted_iota(jnp.int32, (rest, members), 1)
        here_rest = (lane_rest >= first) & (lane_rest < after)
        before_zeros = [jnp.zeros((first, members), BF16)] if first else []
        after_zeros = [jnp.zeros((rest, members), BF16)]

        def trail(point):
            high, low = split(slabs[point])
            wide_high = jnp.concatenate(before_zeros + [high] + after_zeros, axis=0)
            wide_low = jnp.concatenate(before_zeros + [low] + after_zeros, axis=0)
            old = systems[point, after:, :]
            old_high, old_low = split(old)
            change = dot(
                jnp.concatenate([old_high, old_low], axis=1),
                jnp.concatenate([wide_high, wide_high], axis=0),
            ) + dot(old_high, wide_low)
            systems[point, after:, :] = jnp.where(here_rest, 0.0, old) - change

        def trail_many(index, carry):
            for part in range(many):
                trail(index * many + part)
            return carry

        lax.fori_loop(0, points // many, trail_many, 0)

    def finish(point):
        inverse = systems[point]
        right = rights[pl.ds(point, 1), :]
        forward = jnp.sum(inverse * right, axis=1, keepdims=True)
        mean = jnp.sum(inverse * forward, axis=0, keepdims=True)
        own[point, 0:members, :] = (math.sqrt(members - 1.0) * inverse).astype(BF16)
        own[point, members:, :] = jnp.broadcast_to(mean, (META, members)).astype(BF16)

    def finish_many(index, carry):
        for part in range(4):
            finish(index * 4 + part)
        return carry

    lax.fori_loop(0, points // 4, finish_many, 0)
    for index in range(TILES_LON):
        north[index] = own[index]
    for index in range(TILES_LAT):
        east[index] = own[index * TILES_LON]
    corner[0] = own[0]


def solve(labels, arrived):
    slots, rows, members = arrived.shape
    points = TILES_LAT * TILES_LON
    shape = lambda count: jax.ShapeDtypeStruct((count, members + META, members), BF16)
    vmem = pl.BlockSpec(memory_space=pltpu.VMEM)
    return pl.pallas_call(
        solve_kernel,
        out_shape=(shape(points), shape(TILES_LAT), shape(TILES_LON), shape(1)),
        in_specs=[pl.BlockSpec(memory_space=pltpu.SMEM), vmem],
        out_specs=(vmem, vmem, vmem, vmem),
        scratch_shapes=[
            pltpu.VMEM((points * members, members), F32),
            pltpu.VMEM((points, members), F32),
            pltpu.VMEM((2 * BLOCK * BLOCK // members, points, members), F32),
            pltpu.VMEM((points, BLOCK, members), F32),
        ],
        compiler_params=pltpu.CompilerParams(vmem_limit_bytes=48 << 20),
        name="solve",
    )(labels, arrived)


def apply_kernel(
    top, own, east, north, corner, anomalies, flux, out, mean, weights, means, hats
):
    members = anomalies.shape[3]
    cols = anomalies.shape[2]
    tile_row = pl.program_id(1)
    is_top = top[0] == 1
    last = tile_row == TILES_LAT - 1
    half = (FINE + 1) // 2

    def here(col):
        if col < TILES_LON:
            return own[tile_row * TILES_LON + col]
        return east[tile_row]

    def above(col):
        ahead = jnp.minimum(tile_row + 1, TILES_LAT - 1)
        inner = own[ahead * TILES_LON + col] if col < TILES_LON else east[ahead]
        outer = north[col] if col < TILES_LON else corner[0]
        return jnp.where(last & jnp.logical_not(is_top), outer, inner)

    for col in range(TILES_LON + 1):
        low = here(col)
        high = above(col)
        change = (high[:members].astype(F32) - low[:members].astype(F32)).astype(BF16)
        place = slice(col * members, (col + 1) * members)
        weights[0, place, 0:members] = low[:members]
        weights[0, place, members:] = change
        weights[1, place, 0:members] = high[:members]
        weights[1, place, members:] = change
        means[col : col + 1, :] = low[members:].astype(F32)[0:1]
        means[16 + col : 17 + col, :] = high[members:].astype(F32)[0:1]

    width = 32
    offset = lax.broadcasted_iota(jnp.int32, (width, members), 0)
    for part, (start, stop) in enumerate(((0, half), (half, FINE))):
        count = stop - start
        fraction = (
            lax.broadcasted_iota(jnp.int32, (count, width, members), 0) + start
        ).astype(F32) / FINE - part
        carry = None
        for col in range(TILES_LON):
            begin = col * (FINE - 1)
            field = anomalies[0, start:stop, begin : begin + width, :]
            scaled = (field.astype(F32) * fraction).astype(BF16)
            left = jnp.concatenate([field, scaled], axis=2).reshape(count * width, 2 * members)
            place = slice(col * members, (col + 2) * members)
            both = dot(left, weights[part, place, :], NT).reshape(count, width, 2 * members)
            cell = offset - col
            inside = (cell >= 0) & (cell < FINE)
            right_weight = jnp.where(inside, cell.astype(F32) / FINE, 0.0)
            left_weight = jnp.where(inside, 1.0 - cell.astype(F32) / FINE, 0.0)
            result = left_weight * both[:, :, :members] + right_weight * both[:, :, members:]
            head = result[:, 0:8]
            if carry is not None:
                head = head + carry
            carry = result[:, width - 8 :]
            out[0, start:stop, begin : begin + width - 8, :] = jnp.concatenate(
                [head, result[:, 8 : width - 8]], axis=1
            ).astype(BF16)
        out[0, start:stop, cols - 8 :, :] = carry.astype(BF16)

    corner_index = lax.broadcasted_iota(jnp.int32, (16, cols), 0)
    cell = lax.broadcasted_iota(jnp.int32, (16, cols), 1)
    tile = cell // FINE
    part = (cell - tile * FINE).astype(F32) / FINE
    hat = jnp.where(
        tile == corner_index, 1.0 - part, jnp.where(tile + 1 == corner_index, part, 0.0)
    )
    keep = lax.broadcasted_iota(jnp.int32, (16, members), 0) <= TILES_LON
    left = jnp.concatenate(
        [jnp.where(keep, means[0:16, :], 0.0), jnp.where(keep, means[16:32, :], 0.0)], axis=0
    ).astype(BF16)
    for line in range(FINE):
        product = dot(left, anomalies[0, line], NT)
        up = line / FINE
        mixed = (1.0 - up) * product[0:16] + up * product[16:32]
        shift = jnp.sum(mixed * hat, axis=0, keepdims=True)
        place = pl.ds(tile_row * FINE + line, 1)
        mean[0, place, :] = flux[0, place, :] + shift


def apply(top, own, east, north, corner, anomalies, flux):
    lags, rows, cols, members = anomalies.shape
    whole = lambda array: pl.BlockSpec(array.shape, lambda l, r: (0,) * array.ndim)
    strip = pl.BlockSpec((1, FINE, cols, members), lambda l, r: (l, r, 0, 0))
    plane = pl.BlockSpec((1, rows, cols), lambda l, r: (l, 0, 0))
    return pl.pallas_call(
        apply_kernel,
        grid=(lags, TILES_LAT),
        out_shape=(
            jax.ShapeDtypeStruct(anomalies.shape, BF16),
            jax.ShapeDtypeStruct(flux.shape, F32),
        ),
        in_specs=[
            pl.BlockSpec(memory_space=pltpu.SMEM),
            whole(own),
            whole(east),
            whole(north),
            whole(corner),
            strip,
            plane,
        ],
        out_specs=(strip, plane),
        scratch_shapes=[
            pltpu.VMEM((2, (TILES_LON + 1) * members, 2 * members), BF16),
            pltpu.VMEM((32, members), F32),
            pltpu.VMEM((16, cols), F32),
        ],
        compiler_params=pltpu.CompilerParams(vmem_limit_bytes=48 << 20),
        name="apply",
    )(top, own, east, north, corner, anomalies, flux)


def shards(obs_pert, obs_dep, obs_prec, obs_count, owner_point, anomalies, flux_mean):
    lat_devices = lax.axis_size("lat")
    lon_devices = lax.axis_size("lon")
    devices = lat_devices * lon_devices
    holding, locn, members = obs_pert.shape
    capacity = max(1, (holding + devices - 1) // devices)
    columns = TILES_LON * lon_devices
    live = jnp.arange(locn, dtype=jnp.int32)[None, :] < obs_count[:, None]
    weight = jnp.where(live, obs_prec, jnp.zeros((), BF16))
    within = owner_point // columns % TILES_LAT * TILES_LON + owner_point % TILES_LON
    line = lax.broadcasted_iota(jnp.int32, (holding, META, members), 1)
    meta = jnp.where(
        line == 0,
        jnp.concatenate([weight, weight], axis=1)[:, None, :],
        jnp.where(
            line == 1,
            jnp.concatenate([obs_dep, obs_dep], axis=1)[:, None, :],
            within.astype(BF16)[:, None, None],
        ),
    )
    packed = pack(owner_point, obs_pert, meta, columns, lon_devices, devices, capacity)
    arrived = lax.all_to_all(packed, ("lat", "lon"), split_axis=0, concat_axis=0, tiled=True)
    labels = arrived[:, locn + 2, 0].astype(jnp.int32)
    own, east, north, corner = solve(labels, arrived)
    lat_pairs = [(i, i - 1) for i in range(1, lat_devices)]
    lon_pairs = [(i, (i - 1) % lon_devices) for i in range(lon_devices)]
    both_pairs = [
        (a * lon_devices + c, b * lon_devices + d) for a, b in lat_pairs for c, d in lon_pairs
    ]
    east = lax.ppermute(east, "lon", lon_pairs)
    north = lax.ppermute(north, "lat", lat_pairs)
    corner = lax.ppermute(corner, ("lat", "lon"), both_pairs)
    top = (lax.axis_index("lat") == lat_devices - 1).astype(jnp.int32).reshape(1)
    return apply(top, own, east, north, corner, anomalies, flux_mean)


def solution(mesh):
    placed = (
        P(("lat", "lon"), None, None),
        P(("lat", "lon"), None),
        P(("lat", "lon"), None),
        P(("lat", "lon")),
        P(("lat", "lon")),
        P(None, "lat", "lon", None),
        P(None, "lat", "lon"),
    )
    return jax.shard_map(
        shards,
        mesh=mesh,
        in_specs=placed,
        out_specs=(P(None, "lat", "lon", None), P(None, "lat", "lon")),
        check_vma=False,
    )
```

```python
import functools
import math

import jax
import jax.numpy as jnp
from jax import lax
from jax.experimental import pallas as pl
from jax.experimental.pallas import tpu as pltpu
from jax.sharding import PartitionSpec as P

FINE = 25
TILES_LAT = 8
TILES_LON = 8
BLOCK = 16
META = 8
F32 = jnp.float32
BF16 = jnp.bfloat16
NT = (((1,), (1,)), ((), ()))
NN = (((1,), (0,)), ((), ()))


def split(value):
    high = value.astype(BF16)
    return high, (value - high.astype(F32)).astype(BF16)


def dot(left, right, dims=NN):
    return lax.dot_general(left, right, dims, preferred_element_type=F32)


def pack_kernel(
    columns, lon_devices, sent, owner, count, pert, prec, dep, first, second, ranks, weights, departs
):
    holding, locn, members = pert.shape
    devices = first.shape[0] // sent

    @pl.loop(0, devices)
    def _(device):
        ranks[device] = 0

    weights[...] = jnp.concatenate([prec[...], prec[...]], axis=1).astype(F32)
    departs[...] = jnp.concatenate([dep[...], dep[...]], axis=1).astype(F32)
    slots = first.shape[0] + (0 if second is None else second.shape[0])
    if slots > holding:

        @pl.loop(0, first.shape[0])
        def _(slot):
            first[slot, locn:, :] = jnp.full((META, members), -1, BF16)

        if second is not None:

            @pl.loop(0, second.shape[0])
            def _(slot):
                second[slot, locn:, :] = jnp.full((META, members), -1, BF16)

    row = lax.broadcasted_iota(jnp.int32, (META, members), 0)
    slot_of_lane = lax.broadcasted_iota(jnp.int32, (META, members), 1) % locn

    @pl.loop(0, holding)
    def _(block):
        point = owner[block]
        point_row = point // columns
        point_col = point % columns
        device = point_row // TILES_LAT * lon_devices + point_col // TILES_LON
        within = point_row % TILES_LAT * TILES_LON + point_col % TILES_LON
        rank = ranks[device]
        ranks[device] = rank + 1
        weight = jnp.broadcast_to(weights[pl.ds(block, 1), :], (META, members))
        depart = jnp.broadcast_to(departs[pl.ds(block, 1), :], (META, members))
        meta = jnp.where(
            row == 0,
            jnp.where(slot_of_lane < count[block], weight, 0.0),
            jnp.where(row == 1, depart, within.astype(F32)),
        ).astype(BF16)

        def put(out, place):
            out[place, 0:locn, :] = pert[block]
            out[place, locn:, :] = meta

        if second is None:
            put(first, device * sent + jnp.minimum(rank, sent - 1))
        else:
            kept = second.shape[0] // devices

            @pl.when(rank < sent)
            def _():
                put(first, device * sent + rank)

            @pl.when(rank >= sent)
            def _():
                put(second, device * kept + jnp.minimum(rank - sent, kept - 1))


def pack(owner, count, pert, prec, dep, columns, lon_devices, devices, sent, kept):
    holding, locn, members = pert.shape
    shape = lambda each: jax.ShapeDtypeStruct((devices * each, locn + META, members), BF16)
    vmem = pl.BlockSpec(memory_space=pltpu.VMEM)
    smem = pl.BlockSpec(memory_space=pltpu.SMEM)
    kernel = functools.partial(pack_kernel, columns, lon_devices, sent)
    if not kept:
        both = kernel
        kernel = lambda *refs: both(*refs[:6], None, *refs[6:])
    return pl.pallas_call(
        kernel,
        out_shape=(shape(sent), shape(kept)) if kept else (shape(sent),),
        in_specs=[smem, smem, vmem, vmem, vmem],
        out_specs=(vmem, vmem) if kept else (vmem,),
        scratch_shapes=[
            pltpu.SMEM((devices,), jnp.int32),
            pltpu.VMEM((holding, members), F32),
            pltpu.VMEM((holding, members), F32),
        ],
        name="pack",
    )(owner, count, pert, prec, dep)


def label_of(meta):
    return jnp.max(meta.astype(F32)[2:3]).astype(jnp.int32)


def load_systems(arrived, systems, rights):
    slots, rows, members = arrived.shape
    locn = rows - META
    points = rights.shape[0]
    lane = lax.broadcasted_iota(jnp.int32, (members + META, members), 1)
    eye = lax.broadcasted_iota(jnp.int32, (members, members), 0) == lax.broadcasted_iota(
        jnp.int32, (members, members), 1
    )
    ridge = jnp.where(eye, members - 1.0, 0.0)

    def one(slot):
        pert = arrived[slot, 0:locn, :]
        meta = arrived[slot, locn:, :].astype(F32)
        weight = meta[0:1]
        depart = meta[1:2]
        twice = jnp.concatenate([pert, pert], axis=0)
        scaled = twice.T.astype(F32) * weight
        line = jnp.broadcast_to(weight * depart, (META, members))
        left = jnp.concatenate([scaled, line], axis=0)
        high = left.astype(BF16).astype(F32)
        both = jnp.where(lane < locn, high, left - high).astype(BF16)
        gram = dot(both, twice)

        def put(place):
            systems[place] = gram[0:members] + ridge
            rights[pl.ds(place, 1), :] = gram[members : members + 1]

        if slots > points:
            label = label_of(arrived[slot, locn:, :])
            pl.when(label >= 0)(lambda: put(label))
        else:
            put(slot)

    def several(step, carry):
        for part in range(4):
            one(step * 4 + part)
        return carry

    lax.fori_loop(0, slots // 4, several, 0)


def diagonal_inverses(step, systems2d, factors, points, members):
    size = BLOCK
    per = members // size
    lane_block = lax.broadcasted_iota(jnp.int32, (points, members), 1) // size
    rows = []
    for half in range(size // per):
        packed = jnp.zeros((points, members), F32)
        for inner in range(per):
            line = systems2d[pl.ds(size * step + per * half + inner, points, stride=members), :]
            line = pltpu.roll(line, (size * (inner - step)) % members, 1)
            packed = jnp.where(lane_block == inner, line, packed)
        turned = packed.T
        for inner in range(per):
            rows.append(turned[size * inner : size * (inner + 1)])
    sub = lax.broadcasted_iota(jnp.int32, (size, points), 0)
    roots = []
    for k in range(size):
        pivot = jnp.broadcast_to(rows[k][k : k + 1], (size, points))
        root = lax.rsqrt(pivot)
        inverse = root * root
        roots.append(root)
        line = jnp.where(sub == k, 1.0, rows[k])
        scaled = line * inverse
        for i in range(k + 1, size):
            factor = jnp.broadcast_to(rows[i][k : k + 1], (size, points))
            rows[i] = jnp.where(sub == k, 0.0, rows[i]) - factor * scaled
    lower = []
    for i in range(size):
        line = jnp.where(sub < i, rows[i], jnp.where(sub == i, 1.0, 0.0))
        lower.append(line * roots[i])
    whole = []
    for i in range(size):
        total = jnp.zeros((size, points), F32)
        for l in range(i, size):
            total += jnp.broadcast_to(lower[l][i : i + 1], (size, points)) * lower[l]
        whole.append(total)
    for group in range(size // per):
        part = slice(group * per, (group + 1) * per)
        factors[group] = jnp.concatenate(whole[part][::-1], axis=0).T
        factors[size // per + group] = jnp.concatenate(lower[part][::-1], axis=0).T


def solve_kernel(folded, arrived, out, systems2d, rights, factors, slabs):
    points = out.shape[0]
    members = out.shape[2]
    locn = arrived.shape[1] - META
    systems = systems2d.reshape(points, members, members)
    size = BLOCK
    per = members // size
    groups = 2 * size // per
    load_systems(arrived, systems, rights)
    lane8 = lax.broadcasted_iota(jnp.int32, (per, members), 1)
    row = lax.broadcasted_iota(jnp.int32, (members, members), 0) % size
    lane = lax.broadcasted_iota(jnp.int32, (members, members), 1)
    empty = jnp.zeros((members, members), BF16)

    def halves(value):
        high, low = split(value)
        return jnp.concatenate(
            [
                jnp.concatenate([high, low], axis=1),
                jnp.concatenate([high, empty], axis=1),
            ],
            axis=0,
        )

    def product(left, right):
        both = dot(jnp.concatenate(split(left), axis=1), right)
        return both[:, :members] + both[:, members:]

    for step in range(members // size):
        diagonal_inverses(step, systems2d, factors, points, members)
        first = step * size
        after = first + size
        here = (lane >= first) & (lane < after)
        unit = jnp.where(lane - first == row, 1.0, 0.0)

        def small(index):
            start = pl.multiple_of(index * per, per)
            parts = []
            for inner in range(per):
                for group in range(groups):
                    lines = jnp.broadcast_to(
                        factors[group, pl.ds(start + inner, 1), :], (per, members)
                    )
                    lines = pltpu.roll(lines, 0, 1, stride=size, stride_axis=0)
                    lines = pltpu.roll(lines, (size * (inner - per + 1)) % members, 1)
                    parts.append(jnp.where(lane8 // size == inner, lines, 0.0))
            slab = systems[pl.ds(start, per), first:after, :].reshape(members, members)
            right = halves(jnp.where(here, unit, slab))
            both = product(jnp.concatenate(parts, axis=0), right)
            for inner in range(per):
                begin = 2 * size * inner
                slabs[start + inner] = both[begin : begin + size]
                systems[start + inner, first:after, :] = jnp.where(
                    lane[:size] < after, both[begin + size : begin + 2 * size], 0.0
                )

        def small_many(index, carry):
            small(index * 2)
            small(index * 2 + 1)
            return carry

        lax.fori_loop(0, points // per // 2, small_many, 0)
        if after == members:
            continue
        rest = members - after
        lane_rest = lax.broadcasted_iota(jnp.int32, (rest, members), 1)
        here_rest = (lane_rest >= first) & (lane_rest < after)

        def trail(index):
            start = pl.multiple_of(index * per, per)
            right = halves(slabs[pl.ds(start, per)].reshape(members, members))
            parts = []
            for inner in range(per):
                old = systems[start + inner, after:, :]
                moved = pltpu.roll(old, (size * (inner - step)) % members, 1)
                parts.append(jnp.where(lane_rest // size == inner, moved, 0.0))
            change = product(jnp.concatenate(parts, axis=0), right)
            for inner in range(per):
                old = systems[start + inner, after:, :]
                systems[start + inner, after:, :] = (
                    jnp.where(here_rest, 0.0, old) - change[inner * rest : (inner + 1) * rest]
                )

        def trail_many(index, carry):
            trail(index * 2)
            trail(index * 2 + 1)
            return carry

        lax.fori_loop(0, points // per // 2, trail_many, 0)

    def finish(point):
        inverse = systems[point]
        right = rights[pl.ds(point, 1), :]
        forward = jnp.sum(inverse * right, axis=1, keepdims=True)
        mean = jnp.sum(inverse * forward, axis=0, keepdims=True)
        scaled = (math.sqrt(members - 1.0) * inverse).astype(BF16)
        line = jnp.broadcast_to(mean, (META, members))
        if not folded:
            out[point, 0:members, :] = scaled
            out[point, members:, :] = line.astype(BF16)
            return
        upper = scaled[:half]
        turned = jnp.concatenate([upper, upper], axis=0).T.astype(F32)[:half]
        ready = jnp.where(spare, turned, scaled[half:].astype(F32))
        diagonal = jnp.sum(jnp.where(on_diagonal, upper.astype(F32), 0.0), axis=0, keepdims=True)
        label = arrived[point, locn:, :].astype(F32)
        out[point, 0:half, :] = ready.astype(BF16)
        out[point, half:, :] = jnp.where(
            lane8 < 0,
            0.0,
            jnp.where(row8 == 0, line, jnp.where(row8 == 1, diagonal, label)),
        ).astype(BF16)

    half = members // 2
    row_half = lax.broadcasted_iota(jnp.int32, (half, members), 0)
    lane_half = lax.broadcasted_iota(jnp.int32, (half, members), 1)
    spare = lane_half - half > row_half
    on_diagonal = lane_half == row_half
    row8 = lax.broadcasted_iota(jnp.int32, (META, members), 0)

    def finish_many(index, carry):
        for part in range(4):
            finish(index * 4 + part)
        return carry

    lax.fori_loop(0, points // 4, finish_many, 0)


def solve(arrived, points, folded):
    slots, rows, members = arrived.shape
    height = (members // 2 if folded else members) + META
    vmem = pl.BlockSpec(memory_space=pltpu.VMEM)
    return pl.pallas_call(
        functools.partial(solve_kernel, folded),
        out_shape=jax.ShapeDtypeStruct((points, height, members), BF16),
        in_specs=[vmem],
        out_specs=vmem,
        scratch_shapes=[
            pltpu.VMEM((points * members, members), F32),
            pltpu.VMEM((points, members), F32),
            pltpu.VMEM((2 * BLOCK * BLOCK // members, points, members), F32),
            pltpu.VMEM((points, BLOCK, members), F32),
        ],
        compiler_params=pltpu.CompilerParams(vmem_limit_bytes=32 << 20),
        cost_estimate=pl.CostEstimate(
            flops=points * 60_000_000, bytes_accessed=points * 60_000, transcendentals=0
        ),
        name="solve_folded" if folded else "solve",
    )(arrived)


def merge_kernel(kept, *refs):
    if kept:
        solved, origin, folded, own, east, north, corner = refs
    else:
        solved, own, east, north, corner = refs
    members = own.shape[2]
    half = members // 2
    row = lax.broadcasted_iota(jnp.int32, (half, members), 0)
    lane = lax.broadcasted_iota(jnp.int32, (half, members), 1)
    below = lane - half <= row

    def unfolded(step, carry):
        for part in range(4):
            slot = step * 4 + part
            meta = folded[slot, half:, :]
            label = label_of(meta)
            lines = folded[slot, 0:half, :].astype(F32)
            spare = jnp.where(below, 0.0, lines).astype(BF16)
            turned = jnp.concatenate([spare, spare], axis=0).T.astype(F32)[half:]
            upper = jnp.where(
                lane == row,
                jnp.broadcast_to(meta.astype(F32)[1:2], (half, members)),
                jnp.where(lane < half, turned, 0.0),
            )
            own[label, 0:half, :] = upper.astype(BF16)
            own[label, half:members, :] = jnp.where(below, lines, 0.0).astype(BF16)
            own[label, members:, :] = meta
        return carry

    def direct(step, carry):
        for part in range(4):
            slot = step * 4 + part
            label = label_of(origin[slot, origin.shape[1] - META :, :])
            own[label] = solved[slot]
        return carry

    if kept:
        lax.fori_loop(0, solved.shape[0] // 4, direct, 0)
        lax.fori_loop(0, folded.shape[0] // 4, unfolded, 0)
    else:

        @pl.loop(0, own.shape[0])
        def _(label):
            own[label] = solved[label]

    for index in range(TILES_LON):
        north[index] = own[index]
    for index in range(TILES_LAT):
        east[index] = own[index * TILES_LON]
    corner[0] = own[0]


def merge(*arrays):
    members = arrays[0].shape[2]
    shape = lambda count: jax.ShapeDtypeStruct((count, members + META, members), BF16)
    vmem = pl.BlockSpec(memory_space=pltpu.VMEM)
    return pl.pallas_call(
        functools.partial(merge_kernel, len(arrays) > 1),
        out_shape=(shape(TILES_LAT * TILES_LON), shape(TILES_LAT), shape(TILES_LON), shape(1)),
        in_specs=[vmem] * len(arrays),
        out_specs=(vmem,) * 4,
        compiler_params=pltpu.CompilerParams(vmem_limit_bytes=32 << 20),
        name="merge",
    )(*arrays)


def apply_kernel(
    top, own, east, north, corner, anomalies, flux, out, mean, weights, means, hats
):
    members = anomalies.shape[3]
    cols = anomalies.shape[2]
    tile_row = pl.program_id(1)
    is_top = top[0] == 1
    last = tile_row == TILES_LAT - 1
    half = (FINE + 1) // 2

    def here(col):
        if col < TILES_LON:
            return own[tile_row * TILES_LON + col]
        return east[tile_row]

    def above(col):
        ahead = jnp.minimum(tile_row + 1, TILES_LAT - 1)
        inner = own[ahead * TILES_LON + col] if col < TILES_LON else east[ahead]
        outer = north[col] if col < TILES_LON else corner[0]
        return jnp.where(last & jnp.logical_not(is_top), outer, inner)

    for col in range(TILES_LON + 1):
        low = here(col)
        high = above(col)
        change = (high[:members].astype(F32) - low[:members].astype(F32)).astype(BF16)
        place = slice(col * members, (col + 1) * members)
        weights[0, place, 0:members] = low[:members]
        weights[0, place, members:] = change
        weights[1, place, 0:members] = high[:members]
        weights[1, place, members:] = change
        means[col : col + 1, :] = low[members:].astype(F32)[0:1]
        means[16 + col : 17 + col, :] = high[members:].astype(F32)[0:1]

    width = 32
    offset = lax.broadcasted_iota(jnp.int32, (width, members), 0)
    for part, (start, stop) in enumerate(((0, half), (half, FINE))):
        count = stop - start
        fraction = (
            lax.broadcasted_iota(jnp.int32, (count, width, members), 0) + start
        ).astype(F32) / FINE - part
        carry = None
        for col in range(TILES_LON):
            begin = col * (FINE - 1)
            field = anomalies[0, start:stop, begin : begin + width, :]
            scaled = (field.astype(F32) * fraction).astype(BF16)
            left = jnp.concatenate([field, scaled], axis=2).reshape(count * width, 2 * members)
            place = slice(col * members, (col + 2) * members)
            both = dot(left, weights[part, place, :], NT).reshape(count, width, 2 * members)
            cell = offset - col
            inside = (cell >= 0) & (cell < FINE)
            right_weight = jnp.where(inside, cell.astype(F32) / FINE, 0.0)
            left_weight = jnp.where(inside, 1.0 - cell.astype(F32) / FINE, 0.0)
            result = left_weight * both[:, :, :members] + right_weight * both[:, :, members:]
            head = result[:, 0:8]
            if carry is not None:
                head = head + carry
            carry = result[:, width - 8 :]
            out[0, start:stop, begin : begin + width - 8, :] = jnp.concatenate(
                [head, result[:, 8 : width - 8]], axis=1
            ).astype(BF16)
        out[0, start:stop, cols - 8 :, :] = carry.astype(BF16)

    corner_index = lax.broadcasted_iota(jnp.int32, (16, cols), 0)
    cell = lax.broadcasted_iota(jnp.int32, (16, cols), 1)
    tile = cell // FINE
    part = (cell - tile * FINE).astype(F32) / FINE
    hat = jnp.where(
        tile == corner_index, 1.0 - part, jnp.where(tile + 1 == corner_index, part, 0.0)
    )
    keep = lax.broadcasted_iota(jnp.int32, (16, members), 0) <= TILES_LON
    left = jnp.concatenate(
        [jnp.where(keep, means[0:16, :], 0.0), jnp.where(keep, means[16:32, :], 0.0)], axis=0
    ).astype(BF16)
    for line in range(FINE):
        product = dot(left, anomalies[0, line], NT)
        up = line / FINE
        mixed = (1.0 - up) * product[0:16] + up * product[16:32]
        shift = jnp.sum(mixed * hat, axis=0, keepdims=True)
        place = pl.ds(tile_row * FINE + line, 1)
        mean[0, place, :] = flux[0, place, :] + shift


def apply(top, own, east, north, corner, anomalies, flux):
    lags, rows, cols, members = anomalies.shape
    whole = lambda array: pl.BlockSpec(array.shape, lambda l, r: (0,) * array.ndim)
    strip = pl.BlockSpec((1, FINE, cols, members), lambda l, r: (l, r, 0, 0))
    plane = pl.BlockSpec((1, rows, cols), lambda l, r: (l, 0, 0))
    return pl.pallas_call(
        apply_kernel,
        grid=(lags, TILES_LAT),
        out_shape=(
            jax.ShapeDtypeStruct(anomalies.shape, BF16),
            jax.ShapeDtypeStruct(flux.shape, F32),
        ),
        in_specs=[
            pl.BlockSpec(memory_space=pltpu.SMEM),
            whole(own),
            whole(east),
            whole(north),
            whole(corner),
            strip,
            plane,
        ],
        out_specs=(strip, plane),
        scratch_shapes=[
            pltpu.VMEM((2, (TILES_LON + 1) * members, 2 * members), BF16),
            pltpu.VMEM((32, members), F32),
            pltpu.VMEM((16, cols), F32),
        ],
        compiler_params=pltpu.CompilerParams(vmem_limit_bytes=48 << 20),
        name="apply",
    )(top, own, east, north, corner, anomalies, flux)


def shards(obs_pert, obs_dep, obs_prec, obs_count, owner_point, anomalies, flux_mean):
    lat_devices = lax.axis_size("lat")
    lon_devices = lax.axis_size("lon")
    devices = lat_devices * lon_devices
    holding, locn, members = obs_pert.shape
    capacity = max(1, (holding + devices - 1) // devices)
    columns = TILES_LON * lon_devices
    points = TILES_LAT * TILES_LON
    kept = capacity // 2
    sent = capacity - kept
    if devices * capacity > points:
        kept, sent = 0, capacity
    packed = pack(
        owner_point, obs_count, obs_pert, obs_prec, obs_dep, columns, lon_devices, devices, sent, kept
    )
    exchange = functools.partial(
        lax.all_to_all, axis_name=("lat", "lon"), split_axis=0, concat_axis=0, tiled=True
    )
    arrived = exchange(packed[0])
    if kept:
        folded = exchange(solve(packed[1], devices * kept, True))
        solved = solve(arrived, devices * sent, False)
        own, east, north, corner = merge(solved, arrived, folded)
    else:
        own, east, north, corner = merge(solve(arrived, points, False))
    lat_pairs = [(i, i - 1) for i in range(1, lat_devices)]
    lon_pairs = [(i, (i - 1) % lon_devices) for i in range(lon_devices)]
    both_pairs = [
        (a * lon_devices + c, b * lon_devices + d) for a, b in lat_pairs for c, d in lon_pairs
    ]
    east = lax.ppermute(east, "lon", lon_pairs)
    north = lax.ppermute(north, "lat", lat_pairs)
    corner = lax.ppermute(corner, ("lat", "lon"), both_pairs)
    top = (lax.axis_index("lat") == lat_devices - 1).astype(jnp.int32).reshape(1)
    return apply(top, own, east, north, corner, anomalies, flux_mean)


def solution(mesh):
    placed = (
        P(("lat", "lon"), None, None),
        P(("lat", "lon"), None),
        P(("lat", "lon"), None),
        P(("lat", "lon")),
        P(("lat", "lon")),
        P(None, "lat", "lon", None),
        P(None, "lat", "lon"),
    )
    return jax.shard_map(
        shards,
        mesh=mesh,
        in_specs=placed,
        out_specs=(P(None, "lat", "lon", None), P(None, "lat", "lon")),
        check_vma=False,
    )
```

```python
import functools
import math

import jax
import jax.numpy as jnp
from jax import lax
from jax.experimental import pallas as pl
from jax.experimental.pallas import tpu as pltpu
from jax.sharding import PartitionSpec as P

FINE = 25
TILES_LAT = 8
TILES_LON = 8
BLOCK = 16
META = 8
F32 = jnp.float32
BF16 = jnp.bfloat16
NT = (((1,), (1,)), ((), ()))
NN = (((1,), (0,)), ((), ()))


def split(value):
    high = value.astype(BF16)
    return high, (value - high.astype(F32)).astype(BF16)


def dot(left, right, dims=NN):
    return lax.dot_general(left, right, dims, preferred_element_type=F32)


def quotient(value, by):
    if by & (by - 1) == 0:
        return value >> (by.bit_length() - 1), value & (by - 1)
    return lax.div(value, jnp.int32(by)), lax.rem(value, jnp.int32(by))


def place_of(point, columns, lon_devices):
    point_row, point_col = quotient(point, columns)
    device_row, tile_row = quotient(point_row, TILES_LAT)
    device_col, tile_col = quotient(point_col, TILES_LON)
    return device_row * lon_devices + device_col, tile_row * TILES_LON + tile_col


def pack_kernel(columns, lon_devices, capacity, owner, count, pert, prec, dep, *refs):
    outs, (ranks, weights, departs) = refs[:-3], refs[-3:]
    holding, locn, members = pert.shape
    weights[...] = jnp.concatenate([prec[...], prec[...]], axis=1).astype(F32)
    departs[...] = jnp.concatenate([dep[...], dep[...]], axis=1).astype(F32)
    row = lax.broadcasted_iota(jnp.int32, (META, members), 0)
    slot_of_lane = lax.broadcasted_iota(jnp.int32, (META, members), 1) % locn

    def put(out, place, block, within):
        weight = jnp.broadcast_to(weights[pl.ds(block, 1), :], (META, members))
        depart = jnp.broadcast_to(departs[pl.ds(block, 1), :], (META, members))
        out[place, 0:locn, :] = pert[block]
        out[place, locn:, :] = jnp.where(
            row == 0,
            jnp.where(slot_of_lane < count[block], weight, 0.0),
            jnp.where(row == 1, depart, within.astype(F32)),
        ).astype(BF16)

    if len(outs) == 2:
        @pl.loop(0, holding, unroll=4)
        def _(block):
            device, within = place_of(owner[block], columns, lon_devices)
            put(outs[1], device, block, within)
            other = holding - 1 - block
            device, within = place_of(owner[other], columns, lon_devices)
            put(outs[0], device, other, within)

        return

    slots = outs[0].shape[0]

    @pl.loop(0, slots // capacity)
    def _(device):
        ranks[device] = 0

    if slots > holding:

        @pl.loop(0, slots)
        def _(slot):
            outs[0][slot, locn:, :] = jnp.full((META, members), -1, BF16)

    @pl.loop(0, holding)
    def _(block):
        device, within = place_of(owner[block], columns, lon_devices)
        rank = ranks[device]
        ranks[device] = rank + 1
        put(outs[0], device * capacity + jnp.minimum(rank, capacity - 1), block, within)


def pack(owner, count, pert, prec, dep, columns, lon_devices, devices, capacity, halved):
    holding, locn, members = pert.shape
    parts = 2 if halved else 1
    shape = jax.ShapeDtypeStruct((devices * capacity // parts, locn + META, members), BF16)
    vmem = pl.BlockSpec(memory_space=pltpu.VMEM)
    smem = pl.BlockSpec(memory_space=pltpu.SMEM)
    return pl.pallas_call(
        functools.partial(pack_kernel, columns, lon_devices, capacity),
        out_shape=(shape,) * parts,
        in_specs=[smem, smem, vmem, vmem, vmem],
        out_specs=(vmem,) * parts,
        scratch_shapes=[
            pltpu.SMEM((devices,), jnp.int32),
            pltpu.VMEM((holding, members), F32),
            pltpu.VMEM((holding, members), F32),
        ],
        compiler_params=pltpu.CompilerParams(vmem_limit_bytes=12 << 20),
        name="pack",
    )(owner, count, pert, prec, dep)


def label_of(meta):
    return jnp.max(meta.astype(F32)[2:3]).astype(jnp.int32)


def load_systems(arrived, systems, rights):
    slots, rows, members = arrived.shape
    locn = rows - META
    points = rights.shape[0]
    lane = lax.broadcasted_iota(jnp.int32, (members + META, members), 1)
    eye = lax.broadcasted_iota(jnp.int32, (members, members), 0) == lax.broadcasted_iota(
        jnp.int32, (members, members), 1
    )
    ridge = jnp.where(eye, members - 1.0, 0.0)

    def one(slot):
        pert = arrived[slot, 0:locn, :]
        meta = arrived[slot, locn:, :].astype(F32)
        weight = meta[0:1]
        depart = meta[1:2]
        twice = jnp.concatenate([pert, pert], axis=0)
        scaled = twice.T.astype(F32) * weight
        line = jnp.broadcast_to(weight * depart, (META, members))
        left = jnp.concatenate([scaled, line], axis=0)
        high = left.astype(BF16).astype(F32)
        both = jnp.where(lane < locn, high, left - high).astype(BF16)
        gram = dot(both, twice)

        def put(place):
            systems[place] = gram[0:members] + ridge
            rights[pl.ds(place, 1), :] = gram[members : members + 1]

        if slots > points:
            label = label_of(arrived[slot, locn:, :])
            pl.when(label >= 0)(lambda: put(label))
        else:
            put(slot)

    def several(step, carry):
        for part in range(4):
            one(step * 4 + part)
        return carry

    lax.fori_loop(0, slots // 4, several, 0)


def diagonal_inverses(step, systems2d, factors, points, members):
    size = BLOCK
    per = members // size
    lane_block = lax.broadcasted_iota(jnp.int32, (points, members), 1) // size
    rows = []
    for half in range(size // per):
        packed = jnp.zeros((points, members), F32)
        for inner in range(per):
            line = systems2d[pl.ds(size * step + per * half + inner, points, stride=members), :]
            line = pltpu.roll(line, (size * (inner - step)) % members, 1)
            packed = jnp.where(lane_block == inner, line, packed)
        turned = packed.T
        for inner in range(per):
            rows.append(turned[size * inner : size * (inner + 1)])
    sub = lax.broadcasted_iota(jnp.int32, (size, points), 0)
    roots = []
    for k in range(size):
        pivot = jnp.broadcast_to(rows[k][k : k + 1], (size, points))
        root = lax.rsqrt(pivot)
        inverse = root * root
        roots.append(root)
        line = jnp.where(sub == k, 1.0, rows[k])
        scaled = line * inverse
        for i in range(k + 1, size):
            factor = jnp.broadcast_to(rows[i][k : k + 1], (size, points))
            rows[i] = jnp.where(sub == k, 0.0, rows[i]) - factor * scaled
    lower = []
    for i in range(size):
        line = jnp.where(sub < i, rows[i], jnp.where(sub == i, 1.0, 0.0))
        lower.append(line * roots[i])
    whole = []
    for i in range(size):
        total = jnp.zeros((size, points), F32)
        for l in range(i, size):
            total += jnp.broadcast_to(lower[l][i : i + 1], (size, points)) * lower[l]
        whole.append(total)
    for group in range(size // per):
        part = slice(group * per, (group + 1) * per)
        factors[group] = jnp.concatenate(whole[part][::-1], axis=0).T
        factors[size // per + group] = jnp.concatenate(lower[part][::-1], axis=0).T


def solve_kernel(folded, arrived, out, systems2d, rights, factors, slabs):
    points = out.shape[0]
    members = out.shape[2]
    locn = arrived.shape[1] - META
    systems = systems2d.reshape(points, members, members)
    size = BLOCK
    per = members // size
    groups = 2 * size // per
    load_systems(arrived, systems, rights)
    lane8 = lax.broadcasted_iota(jnp.int32, (per, members), 1)
    row = lax.broadcasted_iota(jnp.int32, (members, members), 0) % size
    lane = lax.broadcasted_iota(jnp.int32, (members, members), 1)
    empty = jnp.zeros((members, members), BF16)

    def halves(value):
        high, low = split(value)
        return jnp.concatenate(
            [
                jnp.concatenate([high, low], axis=1),
                jnp.concatenate([high, empty], axis=1),
            ],
            axis=0,
        )

    def product(left, right):
        both = dot(jnp.concatenate(split(left), axis=1), right)
        return both[:, :members] + both[:, members:]

    for step in range(members // size):
        diagonal_inverses(step, systems2d, factors, points, members)
        first = step * size
        after = first + size
        here = (lane >= first) & (lane < after)
        unit = jnp.where(lane - first == row, 1.0, 0.0)

        def small(index):
            start = pl.multiple_of(index * per, per)
            parts = []
            for inner in range(per):
                for group in range(groups):
                    lines = jnp.broadcast_to(
                        factors[group, pl.ds(start + inner, 1), :], (per, members)
                    )
                    lines = pltpu.roll(lines, 0, 1, stride=size, stride_axis=0)
                    lines = pltpu.roll(lines, (size * (inner - per + 1)) % members, 1)
                    parts.append(jnp.where(lane8 // size == inner, lines, 0.0))
            slab = systems[pl.ds(start, per), first:after, :].reshape(members, members)
            right = halves(jnp.where(here, unit, slab))
            both = product(jnp.concatenate(parts, axis=0), right)
            for inner in range(per):
                begin = 2 * size * inner
                slabs[start + inner] = both[begin : begin + size]
                systems[start + inner, first:after, :] = jnp.where(
                    lane[:size] < after, both[begin + size : begin + 2 * size], 0.0
                )

        def small_many(index, carry):
            small(index * 2)
            small(index * 2 + 1)
            return carry

        lax.fori_loop(0, points // per // 2, small_many, 0)
        if after == members:
            continue
        rest = members - after
        lane_rest = lax.broadcasted_iota(jnp.int32, (rest, members), 1)
        here_rest = (lane_rest >= first) & (lane_rest < after)

        def trail(index):
            start = pl.multiple_of(index * per, per)
            right = halves(slabs[pl.ds(start, per)].reshape(members, members))
            parts = []
            for inner in range(per):
                old = systems[start + inner, after:, :]
                moved = pltpu.roll(old, (size * (inner - step)) % members, 1)
                parts.append(jnp.where(lane_rest // size == inner, moved, 0.0))
            change = product(jnp.concatenate(parts, axis=0), right)
            for inner in range(per):
                old = systems[start + inner, after:, :]
                systems[start + inner, after:, :] = (
                    jnp.where(here_rest, 0.0, old) - change[inner * rest : (inner + 1) * rest]
                )

        def trail_many(index, carry):
            trail(index * 2)
            trail(index * 2 + 1)
            return carry

        lax.fori_loop(0, points // per // 2, trail_many, 0)

    def finish(point):
        inverse = systems[point]
        right = rights[pl.ds(point, 1), :]
        forward = jnp.sum(inverse * right, axis=1, keepdims=True)
        mean = jnp.sum(inverse * forward, axis=0, keepdims=True)
        scaled = (math.sqrt(members - 1.0) * inverse).astype(BF16)
        line = jnp.broadcast_to(mean, (META, members))
        if not folded:
            out[point, 0:members, :] = scaled
            out[point, members:, :] = line.astype(BF16)
            return
        upper = scaled[:half]
        turned = jnp.concatenate([upper, upper], axis=0).T.astype(F32)[:half]
        ready = jnp.where(spare, turned, scaled[half:].astype(F32))
        diagonal = jnp.sum(jnp.where(on_diagonal, upper.astype(F32), 0.0), axis=0, keepdims=True)
        label = arrived[point, locn:, :].astype(F32)
        out[point, 0:half, :] = ready.astype(BF16)
        out[point, half:, :] = jnp.where(
            lane8 < 0,
            0.0,
            jnp.where(row8 == 0, line, jnp.where(row8 == 1, diagonal, label)),
        ).astype(BF16)

    half = members // 2
    row_half = lax.broadcasted_iota(jnp.int32, (half, members), 0)
    lane_half = lax.broadcasted_iota(jnp.int32, (half, members), 1)
    spare = lane_half - half > row_half
    on_diagonal = lane_half == row_half
    row8 = lax.broadcasted_iota(jnp.int32, (META, members), 0)

    def finish_many(index, carry):
        for part in range(4):
            finish(index * 4 + part)
        return carry

    lax.fori_loop(0, points // 4, finish_many, 0)


def solve(arrived, points, folded):
    slots, rows, members = arrived.shape
    height = (members // 2 if folded else members) + META
    vmem = pl.BlockSpec(memory_space=pltpu.VMEM)
    return pl.pallas_call(
        functools.partial(solve_kernel, folded),
        out_shape=jax.ShapeDtypeStruct((points, height, members), BF16),
        in_specs=[vmem],
        out_specs=vmem,
        scratch_shapes=[
            pltpu.VMEM((points * members, members), F32),
            pltpu.VMEM((points, members), F32),
            pltpu.VMEM((2 * BLOCK * BLOCK // members, points, members), F32),
            pltpu.VMEM((points, BLOCK, members), F32),
        ],
        compiler_params=pltpu.CompilerParams(vmem_limit_bytes=16 << 20),
        cost_estimate=pl.CostEstimate(
            flops=points * 60_000_000, bytes_accessed=points * 60_000, transcendentals=0
        ),
        name="solve_folded" if folded else "solve",
    )(arrived)


def merge_kernel(kept, *refs):
    if kept:
        solved, origin, folded, own, east, north, corner = refs
    else:
        solved, own, east, north, corner = refs
    members = own.shape[2]
    half = members // 2
    row = lax.broadcasted_iota(jnp.int32, (half, members), 0)
    lane = lax.broadcasted_iota(jnp.int32, (half, members), 1)
    below = lane - half <= row

    def unfolded(step, carry):
        for part in range(4):
            slot = step * 4 + part
            meta = folded[slot, half:, :]
            label = label_of(meta)
            lines = folded[slot, 0:half, :].astype(F32)
            spare = jnp.where(below, 0.0, lines).astype(BF16)
            turned = jnp.concatenate([spare, spare], axis=0).T.astype(F32)[half:]
            upper = jnp.where(
                lane == row,
                jnp.broadcast_to(meta.astype(F32)[1:2], (half, members)),
                jnp.where(lane < half, turned, 0.0),
            )
            own[label, 0:half, :] = upper.astype(BF16)
            own[label, half:members, :] = jnp.where(below, lines, 0.0).astype(BF16)
            own[label, members:, :] = meta
        return carry

    def direct(step, carry):
        for part in range(4):
            slot = step * 4 + part
            label = label_of(origin[slot, origin.shape[1] - META :, :])
            own[label] = solved[slot]
        return carry

    if kept:
        lax.fori_loop(0, solved.shape[0] // 4, direct, 0)
        lax.fori_loop(0, folded.shape[0] // 4, unfolded, 0)
    else:

        @pl.loop(0, own.shape[0])
        def _(label):
            own[label] = solved[label]

    for index in range(TILES_LON):
        north[index] = own[index]
    for index in range(TILES_LAT):
        east[index] = own[index * TILES_LON]
    corner[0] = own[0]


def merge(*arrays):
    members = arrays[0].shape[2]
    shape = lambda count: jax.ShapeDtypeStruct((count, members + META, members), BF16)
    vmem = pl.BlockSpec(memory_space=pltpu.VMEM)
    return pl.pallas_call(
        functools.partial(merge_kernel, len(arrays) > 1),
        out_shape=(shape(TILES_LAT * TILES_LON), shape(TILES_LAT), shape(TILES_LON), shape(1)),
        in_specs=[vmem] * len(arrays),
        out_specs=(vmem,) * 4,
        compiler_params=pltpu.CompilerParams(vmem_limit_bytes=16 << 20),
        name="merge",
    )(*arrays)


def apply_kernel(
    top, own, east, north, corner, anomalies, flux, out, mean, weights, means, hats
):
    members = anomalies.shape[3]
    cols = anomalies.shape[2]
    tile_row = pl.program_id(1)
    is_top = top[0] == 1
    last = tile_row == TILES_LAT - 1
    half = (FINE + 1) // 2

    def here(col):
        if col < TILES_LON:
            return own[tile_row * TILES_LON + col]
        return east[tile_row]

    def above(col):
        ahead = jnp.minimum(tile_row + 1, TILES_LAT - 1)
        inner = own[ahead * TILES_LON + col] if col < TILES_LON else east[ahead]
        outer = north[col] if col < TILES_LON else corner[0]
        return jnp.where(last & jnp.logical_not(is_top), outer, inner)

    for col in range(TILES_LON + 1):
        low = here(col)
        high = above(col)
        change = high[:members].astype(F32) - low[:members].astype(F32)
        change = (change * (1.0 / FINE)).astype(BF16)
        place = slice(col * members, (col + 1) * members)
        weights[0, place, 0:members] = low[:members]
        weights[0, place, members:] = change
        weights[1, place, 0:members] = high[:members]
        weights[1, place, members:] = change
        means[col : col + 1, :] = low[members:].astype(F32)[0:1]
        means[16 + col : 17 + col, :] = high[members:].astype(F32)[0:1]

    width = 32
    offset = lax.broadcasted_iota(jnp.int32, (width, members), 0)
    for part, (start, stop) in enumerate(((0, half), (half, FINE))):
        count = stop - start
        number = jnp.concatenate(
            [jnp.full((1, width, members), line - part * FINE, BF16) for line in range(start, stop)]
        )
        carry = None
        for col in range(TILES_LON):
            begin = col * (FINE - 1)
            field = anomalies[0, start:stop, begin : begin + width, :]
            scaled = field * number
            left = jnp.concatenate([field, scaled], axis=2).reshape(count * width, 2 * members)
            place = slice(col * members, (col + 2) * members)
            both = dot(left, weights[part, place, :], NT).reshape(count, width, 2 * members)
            cell = offset - col
            inside = (cell >= 0) & (cell < FINE)
            right_weight = jnp.where(inside, cell.astype(F32) / FINE, 0.0)
            left_weight = jnp.where(inside, 1.0 - cell.astype(F32) / FINE, 0.0)
            result = left_weight * both[:, :, :members] + right_weight * both[:, :, members:]
            head = result[:, 0:8]
            if carry is not None:
                head = head + carry
            carry = result[:, width - 8 :]
            out[0, start:stop, begin : begin + width - 8, :] = jnp.concatenate(
                [head, result[:, 8 : width - 8]], axis=1
            ).astype(BF16)
        out[0, start:stop, cols - 8 :, :] = carry.astype(BF16)

    corner_index = lax.broadcasted_iota(jnp.int32, (16, cols), 0)
    cell = lax.broadcasted_iota(jnp.int32, (16, cols), 1)
    tile = cell // FINE
    part = (cell - tile * FINE).astype(F32) / FINE
    hat = jnp.where(
        tile == corner_index, 1.0 - part, jnp.where(tile + 1 == corner_index, part, 0.0)
    )
    keep = lax.broadcasted_iota(jnp.int32, (16, members), 0) <= TILES_LON
    left = jnp.concatenate(
        [jnp.where(keep, means[0:16, :], 0.0), jnp.where(keep, means[16:32, :], 0.0)], axis=0
    ).astype(BF16)
    for line in range(FINE):
        product = dot(left, anomalies[0, line], NT)
        up = line / FINE
        mixed = (1.0 - up) * product[0:16] + up * product[16:32]
        shift = jnp.sum(mixed * hat, axis=0, keepdims=True)
        place = pl.ds(tile_row * FINE + line, 1)
        mean[0, place, :] = flux[0, place, :] + shift


def apply(top, own, east, north, corner, anomalies, flux):
    lags, rows, cols, members = anomalies.shape
    whole = lambda array: pl.BlockSpec(array.shape, lambda l, r: (0,) * array.ndim)
    strip = pl.BlockSpec((1, FINE, cols, members), lambda l, r: (l, r, 0, 0))
    plane = pl.BlockSpec((1, rows, cols), lambda l, r: (l, 0, 0))
    return pl.pallas_call(
        apply_kernel,
        grid=(lags, TILES_LAT),
        out_shape=(
            jax.ShapeDtypeStruct(anomalies.shape, BF16),
            jax.ShapeDtypeStruct(flux.shape, F32),
        ),
        in_specs=[
            pl.BlockSpec(memory_space=pltpu.SMEM),
            whole(own),
            whole(east),
            whole(north),
            whole(corner),
            strip,
            plane,
        ],
        out_specs=(strip, plane),
        scratch_shapes=[
            pltpu.VMEM((2, (TILES_LON + 1) * members, 2 * members), BF16),
            pltpu.VMEM((32, members), F32),
            pltpu.VMEM((16, cols), F32),
        ],
        compiler_params=pltpu.CompilerParams(vmem_limit_bytes=32 << 20),
        name="apply",
    )(top, own, east, north, corner, anomalies, flux)


def shards(obs_pert, obs_dep, obs_prec, obs_count, owner_point, anomalies, flux_mean):
    lat_devices = lax.axis_size("lat")
    lon_devices = lax.axis_size("lon")
    devices = lat_devices * lon_devices
    holding, locn, members = obs_pert.shape
    capacity = max(1, (holding + devices - 1) // devices)
    columns = TILES_LON * lon_devices
    points = TILES_LAT * TILES_LON
    halved = capacity == 2 and devices * capacity == holding == points
    packed = pack(
        owner_point, obs_count, obs_pert, obs_prec, obs_dep,
        columns, lon_devices, devices, capacity, halved,
    )
    exchange = functools.partial(
        lax.all_to_all, axis_name=("lat", "lon"), split_axis=0, concat_axis=0, tiled=True
    )
    arrived = exchange(packed[0])
    if halved:
        folded = exchange(solve(packed[1], points // 2, True))
        solved = solve(arrived, points // 2, False)
        own, east, north, corner = merge(solved, arrived, folded)
    else:
        own, east, north, corner = merge(solve(arrived, points, False))
    lat_pairs = [(i, i - 1) for i in range(1, lat_devices)]
    lon_pairs = [(i, (i - 1) % lon_devices) for i in range(lon_devices)]
    both_pairs = [
        (a * lon_devices + c, b * lon_devices + d) for a, b in lat_pairs for c, d in lon_pairs
    ]
    east = lax.ppermute(east, "lon", lon_pairs)
    north = lax.ppermute(north, "lat", lat_pairs)
    corner = lax.ppermute(corner, ("lat", "lon"), both_pairs)
    top = (lax.axis_index("lat") == lat_devices - 1).astype(jnp.int32).reshape(1)
    return apply(top, own, east, north, corner, anomalies, flux_mean)


def solution(mesh):
    placed = (
        P(("lat", "lon"), None, None),
        P(("lat", "lon"), None),
        P(("lat", "lon"), None),
        P(("lat", "lon")),
        P(("lat", "lon")),
        P(None, "lat", "lon", None),
        P(None, "lat", "lon"),
    )
    return jax.shard_map(
        shards,
        mesh=mesh,
        in_specs=placed,
        out_specs=(P(None, "lat", "lon", None), P(None, "lat", "lon")),
        check_vma=False,
    )
```

```python
import functools
import math

import jax
import jax.numpy as jnp
from jax import lax
from jax.experimental import pallas as pl
from jax.experimental.pallas import tpu as pltpu
from jax.sharding import PartitionSpec as P

FINE = 25
TILES_LAT = 8
TILES_LON = 8
BLOCK = 16
META = 8
F32 = jnp.float32
BF16 = jnp.bfloat16
NT = (((1,), (1,)), ((), ()))
NN = (((1,), (0,)), ((), ()))


def split(value):
    high = value.astype(BF16)
    return high, (value - high.astype(F32)).astype(BF16)


def dot(left, right, dims=NN):
    return lax.dot_general(left, right, dims, preferred_element_type=F32)


def quotient(value, by):
    if by & (by - 1) == 0:
        return value >> (by.bit_length() - 1), value & (by - 1)
    return lax.div(value, jnp.int32(by)), lax.rem(value, jnp.int32(by))


def place_of(point, columns, lon_devices):
    point_row, point_col = quotient(point, columns)
    device_row, tile_row = quotient(point_row, TILES_LAT)
    device_col, tile_col = quotient(point_col, TILES_LON)
    return device_row * lon_devices + device_col, tile_row * TILES_LON + tile_col


def pack_kernel(columns, lon_devices, capacity, owner, count, pert, prec, dep, *refs):
    outs, (ranks, weights, departs) = refs[:-3], refs[-3:]
    holding, locn, members = pert.shape
    weights[...] = jnp.concatenate([prec[...], prec[...]], axis=1).astype(F32)
    departs[...] = jnp.concatenate([dep[...], dep[...]], axis=1).astype(F32)
    row = lax.broadcasted_iota(jnp.int32, (META, members), 0)
    slot_of_lane = lax.broadcasted_iota(jnp.int32, (META, members), 1) % locn

    def put(out, place, block, within):
        weight = jnp.broadcast_to(weights[pl.ds(block, 1), :], (META, members))
        depart = jnp.broadcast_to(departs[pl.ds(block, 1), :], (META, members))
        out[place, 0:locn, :] = pert[block]
        out[place, locn:, :] = jnp.where(
            row == 0,
            jnp.where(slot_of_lane < count[block], weight, 0.0),
            jnp.where(row == 1, depart, within.astype(F32)),
        ).astype(BF16)

    if len(outs) == 2:
        @pl.loop(0, holding, unroll=4)
        def _(block):
            device, within = place_of(owner[block], columns, lon_devices)
            put(outs[1], device, block, within)
            other = holding - 1 - block
            device, within = place_of(owner[other], columns, lon_devices)
            put(outs[0], device, other, within)

        return

    slots = outs[0].shape[0]

    @pl.loop(0, slots // capacity)
    def _(device):
        ranks[device] = 0

    if slots > holding:

        @pl.loop(0, slots)
        def _(slot):
            outs[0][slot, locn:, :] = jnp.full((META, members), -1, BF16)

    @pl.loop(0, holding)
    def _(block):
        device, within = place_of(owner[block], columns, lon_devices)
        rank = ranks[device]
        ranks[device] = rank + 1
        put(outs[0], device * capacity + jnp.minimum(rank, capacity - 1), block, within)


def pack(owner, count, pert, prec, dep, columns, lon_devices, devices, capacity, halved):
    holding, locn, members = pert.shape
    parts = 2 if halved else 1
    shape = jax.ShapeDtypeStruct((devices * capacity // parts, locn + META, members), BF16)
    vmem = pl.BlockSpec(memory_space=pltpu.VMEM)
    smem = pl.BlockSpec(memory_space=pltpu.SMEM)
    return pl.pallas_call(
        functools.partial(pack_kernel, columns, lon_devices, capacity),
        out_shape=(shape,) * parts,
        in_specs=[smem, smem, vmem, vmem, vmem],
        out_specs=(vmem,) * parts,
        scratch_shapes=[
            pltpu.SMEM((devices,), jnp.int32),
            pltpu.VMEM((holding, members), F32),
            pltpu.VMEM((holding, members), F32),
        ],
        name="pack",
    )(owner, count, pert, prec, dep)


def label_of(meta):
    return jnp.max(meta.astype(F32)[2:3]).astype(jnp.int32)


def load_systems(arrived, systems, rights):
    slots, rows, members = arrived.shape
    locn = rows - META
    points = rights.shape[0]
    lane = lax.broadcasted_iota(jnp.int32, (members + META, members), 1)
    eye = lax.broadcasted_iota(jnp.int32, (members, members), 0) == lax.broadcasted_iota(
        jnp.int32, (members, members), 1
    )
    ridge = jnp.where(eye, members - 1.0, 0.0)

    def one(slot):
        pert = arrived[slot, 0:locn, :]
        meta = arrived[slot, locn:, :].astype(F32)
        weight = meta[0:1]
        depart = meta[1:2]
        twice = jnp.concatenate([pert, pert], axis=0)
        scaled = twice.T.astype(F32) * weight
        line = jnp.broadcast_to(weight * depart, (META, members))
        left = jnp.concatenate([scaled, line], axis=0)
        high = left.astype(BF16).astype(F32)
        both = jnp.where(lane < locn, high, left - high).astype(BF16)
        gram = dot(both, twice)

        def put(place):
            systems[place] = gram[0:members] + ridge
            rights[pl.ds(place, 1), :] = gram[members : members + 1]

        if slots > points:
            label = label_of(arrived[slot, locn:, :])
            pl.when(label >= 0)(lambda: put(label))
        else:
            put(slot)

    def several(step, carry):
        for part in range(8):
            one(step * 8 + part)
        return carry

    lax.fori_loop(0, slots // 8, several, 0)


def diagonal_inverses(step, systems2d, factors, points, members):
    size = BLOCK
    per = members // size
    lane_block = lax.broadcasted_iota(jnp.int32, (points, members), 1) // size
    rows = []
    for half in range(size // per):
        packed = jnp.zeros((points, members), F32)
        for inner in range(per):
            line = systems2d[pl.ds(size * step + per * half + inner, points, stride=members), :]
            line = pltpu.roll(line, (size * (inner - step)) % members, 1)
            packed = jnp.where(lane_block == inner, line, packed)
        turned = packed.T
        for inner in range(per):
            rows.append(turned[size * inner : size * (inner + 1)])
    half = size // 2
    sub = lax.broadcasted_iota(jnp.int32, (half, points), 0)
    rows = [[line[:half], line[half:]] for line in rows]
    spread = lambda line, k: jnp.broadcast_to(
        line[k // half][k % half : k % half + 1], (half, points)
    )
    roots = []
    for k in range(size):
        part = k // half
        root = lax.rsqrt(spread(rows[k], k))
        inverse = root * root
        roots.append(root)
        factors_k = [spread(rows[k], i) for i in range(k + 1, size)]
        line = list(rows[k])
        line[part] = jnp.where(sub == k % half, 1.0, line[part])
        line = [piece * inverse for piece in line]
        for i in range(k + 1, size):
            rows[i][part] = jnp.where(sub == k % half, 0.0, rows[i][part])
            rows[i] = [old - factors_k[i - k - 1] * piece for old, piece in zip(rows[i], line)]
    lower = []
    for i in range(size):
        part = i // half
        line = [piece * roots[i] for piece in rows[i][: part + 1]]
        line[part] = jnp.where(
            sub < i % half, line[part], jnp.where(sub == i % half, roots[i], 0.0)
        )
        lower.append(line)
    nothing = jnp.zeros((half, points), F32)
    whole = []
    for i in range(size):
        total = [nothing, nothing]
        for l in range(i, size):
            factor = spread(lower[l], i)
            for piece in range(l // half + 1):
                term = factor * lower[l][piece]
                total[piece] = term if l == i or (piece and l == half) else total[piece] + term
        whole.append(jnp.concatenate(total, axis=0))
    lower = [jnp.concatenate((line + [nothing])[:2], axis=0) for line in lower]
    for group in range(size // per):
        part = slice(group * per, (group + 1) * per)
        factors[group] = jnp.concatenate(whole[part][::-1], axis=0).T
        factors[size // per + group] = jnp.concatenate(lower[part][::-1], axis=0).T


def solve_kernel(folded, arrived, out, systems2d, rights, factors, slabs):
    points = out.shape[0]
    members = out.shape[2]
    locn = arrived.shape[1] - META
    systems = systems2d.reshape(points, members, members)
    size = BLOCK
    per = members // size
    groups = 2 * size // per
    load_systems(arrived, systems, rights)
    lane8 = lax.broadcasted_iota(jnp.int32, (per, members), 1)
    row = lax.broadcasted_iota(jnp.int32, (members, members), 0) % size
    lane = lax.broadcasted_iota(jnp.int32, (members, members), 1)
    empty = jnp.zeros((members, members), BF16)

    def halves(value):
        high, low = split(value)
        return jnp.concatenate(
            [
                jnp.concatenate([high, low], axis=1),
                jnp.concatenate([high, empty], axis=1),
            ],
            axis=0,
        )

    def product(left, right):
        both = dot(jnp.concatenate(split(left), axis=1), right)
        return both[:, :members] + both[:, members:]

    diagonal_inverses(0, systems2d, factors, points, members)
    for step in range(members // size):
        first = step * size
        after = first + size
        here = (lane >= first) & (lane < after)
        unit = jnp.where(lane - first == row, 1.0, 0.0)

        def small(index):
            start = index * per
            parts = []
            for inner in range(per):
                for group in range(groups):
                    lines = jnp.broadcast_to(
                        factors[group, pl.ds(start + inner, 1), :], (per, members)
                    )
                    move = (size * (inner - per + 1)) % members
                    direct = move if move <= size else 0
                    lines = pltpu.roll(lines, direct, 1, stride=size, stride_axis=0)
                    if move != direct:
                        lines = pltpu.roll(lines, move, 1)
                    parts.append(jnp.where(lane8 // size == inner, lines, 0.0))
            slab = systems[pl.ds(start, per), first:after, :].reshape(members, members)
            right = halves(jnp.where(here, unit, slab))
            both = product(jnp.concatenate(parts, axis=0), right)
            for inner in range(per):
                begin = 2 * size * inner
                slabs[start + inner] = both[begin : begin + size]
                systems[start + inner, first:after, :] = jnp.where(
                    lane[:size] < after, both[begin + size : begin + 2 * size], 0.0
                )

        for index in range(points // per):
            small(index)
        if after == members:
            continue
        def trail(index, begin, stop):
            start = index * per
            rest = stop - begin
            lane_rest = lax.broadcasted_iota(jnp.int32, (rest, members), 1)
            here_rest = (lane_rest >= first) & (lane_rest < after)
            right = halves(slabs[pl.ds(start, per)].reshape(members, members))
            parts = []
            for inner in range(per):
                old = systems[start + inner, begin:stop, :]
                moved = pltpu.roll(old, (size * (inner - step)) % members, 1)
                parts.append(jnp.where(lane_rest // size == inner, moved, 0.0))
            change = product(jnp.concatenate(parts, axis=0), right)
            for inner in range(per):
                old = systems[start + inner, begin:stop, :]
                systems[start + inner, begin:stop, :] = (
                    jnp.where(here_rest, 0.0, old) - change[inner * rest : (inner + 1) * rest]
                )

        for index in range(points // per):
            trail(index, after, after + size)
        diagonal_inverses(step + 1, systems2d, factors, points, members)
        if after + size < members:
            for index in range(points // per):
                trail(index, after + size, members)

    def finish(point):
        inverse = systems[point]
        right = rights[pl.ds(point, 1), :]
        forward = jnp.sum(inverse * right, axis=1, keepdims=True)
        mean = jnp.sum(inverse * forward, axis=0, keepdims=True)
        scaled = (math.sqrt(members - 1.0) * inverse).astype(BF16)
        line = jnp.broadcast_to(mean, (META, members))
        if not folded:
            out[point, 0:members, :] = scaled
            out[point, members:, :] = line.astype(BF16)
            return
        upper = scaled[:half]
        turned = jnp.concatenate([upper, upper], axis=0).T.astype(F32)[:half]
        ready = jnp.where(spare, turned, scaled[half:].astype(F32))
        diagonal = jnp.sum(jnp.where(on_diagonal, upper.astype(F32), 0.0), axis=0, keepdims=True)
        label = arrived[point, locn:, :].astype(F32)
        out[point, 0:half, :] = ready.astype(BF16)
        out[point, half:, :] = jnp.where(
            lane8 < 0,
            0.0,
            jnp.where(row8 == 0, line, jnp.where(row8 == 1, diagonal, label)),
        ).astype(BF16)

    half = members // 2
    row_half = lax.broadcasted_iota(jnp.int32, (half, members), 0)
    lane_half = lax.broadcasted_iota(jnp.int32, (half, members), 1)
    spare = lane_half - half > row_half
    on_diagonal = lane_half == row_half
    row8 = lax.broadcasted_iota(jnp.int32, (META, members), 0)

    def finish_many(index, carry):
        for part in range(8):
            finish(index * 8 + part)
        return carry

    lax.fori_loop(0, points // 8, finish_many, 0)


def solve(arrived, points, folded):
    slots, rows, members = arrived.shape
    height = (members // 2 if folded else members) + META
    vmem = pl.BlockSpec(memory_space=pltpu.VMEM)
    return pl.pallas_call(
        functools.partial(solve_kernel, folded),
        out_shape=jax.ShapeDtypeStruct((points, height, members), BF16),
        in_specs=[vmem],
        out_specs=vmem,
        scratch_shapes=[
            pltpu.VMEM((points * members, members), F32),
            pltpu.VMEM((points, members), F32),
            pltpu.VMEM((2 * BLOCK * BLOCK // members, points, members), F32),
            pltpu.VMEM((points, BLOCK, members), F32),
        ],
        cost_estimate=pl.CostEstimate(
            flops=points * 60_000_000, bytes_accessed=points * 60_000, transcendentals=0
        ),
        name="solve_folded" if folded else "solve",
    )(arrived)


def merge_kernel(kept, *refs):
    if kept:
        solved, origin, folded, own, east, north, corner = refs
    else:
        solved, own, east, north, corner = refs
    members = own.shape[2]
    half = members // 2
    row = lax.broadcasted_iota(jnp.int32, (half, members), 0)
    lane = lax.broadcasted_iota(jnp.int32, (half, members), 1)
    below = lane - half <= row

    def unfolded(step, carry):
        for part in range(4):
            slot = step * 4 + part
            meta = folded[slot, half:, :]
            label = label_of(meta)
            lines = folded[slot, 0:half, :].astype(F32)
            spare = jnp.where(below, 0.0, lines).astype(BF16)
            turned = jnp.concatenate([spare, spare], axis=0).T.astype(F32)[half:]
            upper = jnp.where(
                lane == row,
                jnp.broadcast_to(meta.astype(F32)[1:2], (half, members)),
                jnp.where(lane < half, turned, 0.0),
            )
            own[label, 0:half, :] = upper.astype(BF16)
            own[label, half:members, :] = jnp.where(below, lines, 0.0).astype(BF16)
            own[label, members:, :] = meta
        return carry

    def direct(step, carry):
        for part in range(4):
            slot = step * 4 + part
            label = label_of(origin[slot, origin.shape[1] - META :, :])
            own[label] = solved[slot]
        return carry

    if kept:
        lax.fori_loop(0, solved.shape[0] // 4, direct, 0)
        lax.fori_loop(0, folded.shape[0] // 4, unfolded, 0)
    else:

        @pl.loop(0, own.shape[0])
        def _(label):
            own[label] = solved[label]

    for index in range(TILES_LON):
        north[index] = own[index]
    for index in range(TILES_LAT):
        east[index] = own[index * TILES_LON]
    corner[0] = own[0]


def merge(*arrays):
    members = arrays[0].shape[2]
    shape = lambda count: jax.ShapeDtypeStruct((count, members + META, members), BF16)
    vmem = pl.BlockSpec(memory_space=pltpu.VMEM)
    return pl.pallas_call(
        functools.partial(merge_kernel, len(arrays) > 1),
        out_shape=(shape(TILES_LAT * TILES_LON), shape(TILES_LAT), shape(TILES_LON), shape(1)),
        in_specs=[vmem] * len(arrays),
        out_specs=(vmem,) * 4,
        name="merge",
    )(*arrays)


def apply_kernel(first, *refs):
    last = first == TILES_LAT - 1
    if last:
        top, own, east, north, corner, anomalies, flux, _, before, *refs = refs
    else:
        own, east, anomalies, flux, *refs = refs
    out, mean, weights, means = refs
    members = anomalies.shape[3]
    cols = anomalies.shape[2]
    tile_row = pl.program_id(1) + first
    if last:
        mean[...] = before[...]

    def inner(row, col):
        return own[row * TILES_LON + col] if col < TILES_LON else east[row]

    def here(col):
        return inner(tile_row, col)

    def above(col):
        if not last:
            return inner(tile_row + 1, col)
        outer = north[col] if col < TILES_LON else corner[0]
        return jnp.where(top[0] == 1, inner(TILES_LAT - 1, col), outer)

    half = (FINE + 1) // 2

    for col in range(TILES_LON + 1):
        low = here(col)
        high = above(col)
        change = high[:members].astype(F32) - low[:members].astype(F32)
        change = (change * (1.0 / FINE)).astype(BF16)
        place = slice(col * members, (col + 1) * members)
        weights[0, place, 0:members] = low[:members]
        weights[0, place, members:] = change
        weights[1, place, 0:members] = high[:members]
        weights[1, place, members:] = change
        means[col : col + 1, :] = low[members:].astype(F32)[0:1]
        means[16 + col : 17 + col, :] = high[members:].astype(F32)[0:1]

    width = 32
    offset = lax.broadcasted_iota(jnp.int32, (width, members), 0)
    for part, (start, stop) in enumerate(((0, half), (half, FINE))):
        count = stop - start
        number = jnp.concatenate(
            [jnp.full((1, width, members), line - part * FINE, BF16) for line in range(start, stop)]
        )
        carry = None
        for col in range(TILES_LON):
            begin = col * (FINE - 1)
            field = anomalies[0, start:stop, begin : begin + width, :]
            scaled = field * number
            left = jnp.concatenate([field, scaled], axis=2).reshape(count * width, 2 * members)
            place = slice(col * members, (col + 2) * members)
            both = dot(left, weights[part, place, :], NT).reshape(count, width, 2 * members)
            cell = offset - col
            inside = (cell >= 0) & (cell < FINE)
            right_weight = jnp.where(inside, cell.astype(F32) / FINE, 0.0)
            left_weight = jnp.where(inside, 1.0 - cell.astype(F32) / FINE, 0.0)
            result = left_weight * both[:, :, :members] + right_weight * both[:, :, members:]
            head = result[:, 0:8]
            if carry is not None:
                head = head + carry
            carry = result[:, width - 8 :]
            out[0, start:stop, begin : begin + width - 8, :] = jnp.concatenate(
                [head, result[:, 8 : width - 8]], axis=1
            ).astype(BF16)
        out[0, start:stop, cols - 8 :, :] = carry.astype(BF16)

    corner_index = lax.broadcasted_iota(jnp.int32, (16, cols), 0)
    cell = lax.broadcasted_iota(jnp.int32, (16, cols), 1)
    tile = cell // FINE
    part = (cell - tile * FINE).astype(F32) / FINE
    hat = jnp.where(
        tile == corner_index, 1.0 - part, jnp.where(tile + 1 == corner_index, part, 0.0)
    )
    keep = lax.broadcasted_iota(jnp.int32, (16, members), 0) <= TILES_LON
    left = jnp.concatenate(
        [jnp.where(keep, means[0:16, :], 0.0), jnp.where(keep, means[16:32, :], 0.0)], axis=0
    ).astype(BF16)
    for line in range(FINE):
        product = dot(left, anomalies[0, line], NT)
        up = line / FINE
        mixed = (1.0 - up) * product[0:16] + up * product[16:32]
        shift = jnp.sum(mixed * hat, axis=0, keepdims=True)
        place = pl.ds(tile_row * FINE + line, 1)
        mean[0, place, :] = flux[0, place, :] + shift


def apply(first, count, operands, anomalies, flux, earlier=()):
    lags, rows, cols, members = anomalies.shape
    whole = lambda array: pl.BlockSpec(array.shape, lambda l, r: (0,) * array.ndim)
    strip = pl.BlockSpec((1, FINE, cols, members), lambda l, r: (l, r + first, 0, 0))
    plane = pl.BlockSpec((1, rows, cols), lambda l, r: (l, 0, 0))
    specs = [
        pl.BlockSpec(memory_space=pltpu.SMEM) if array.ndim == 1 else whole(array)
        for array in operands
    ] + [strip, plane]
    aliases = {}
    if earlier:
        aliases = {len(specs): 0, len(specs) + 1: 1}
        specs += [pl.BlockSpec(memory_space=pl.ANY), plane]
    cells = count * FINE * cols * lags
    return pl.pallas_call(
        functools.partial(apply_kernel, first),
        grid=(lags, count),
        out_shape=(
            jax.ShapeDtypeStruct(anomalies.shape, BF16),
            jax.ShapeDtypeStruct(flux.shape, F32),
        ),
        in_specs=specs,
        out_specs=(strip, plane),
        scratch_shapes=[
            pltpu.VMEM((2, (TILES_LON + 1) * members, 2 * members), BF16),
            pltpu.VMEM((32, members), F32),
        ],
        input_output_aliases=aliases,
        cost_estimate=pl.CostEstimate(
            flops=cells * members * members * 8,
            bytes_accessed=cells * members * 4,
            transcendentals=0,
        ),
        name="apply_last" if earlier else "apply",
    )(*operands, anomalies, flux, *earlier)


def shards(obs_pert, obs_dep, obs_prec, obs_count, owner_point, anomalies, flux_mean):
    lat_devices = lax.axis_size("lat")
    lon_devices = lax.axis_size("lon")
    devices = lat_devices * lon_devices
    holding, locn, members = obs_pert.shape
    capacity = max(1, (holding + devices - 1) // devices)
    columns = TILES_LON * lon_devices
    points = TILES_LAT * TILES_LON
    halved = capacity == 2 and devices * capacity == holding == points
    packed = pack(
        owner_point, obs_count, obs_pert, obs_prec, obs_dep,
        columns, lon_devices, devices, capacity, halved,
    )
    exchange = functools.partial(
        lax.all_to_all, axis_name=("lat", "lon"), split_axis=0, concat_axis=0, tiled=True
    )
    arrived = exchange(packed[0])
    if halved:
        folded = exchange(solve(packed[1], points // 2, True))
        solved = solve(arrived, points // 2, False)
        own, east, north, corner = merge(solved, arrived, folded)
    else:
        own, east, north, corner = merge(solve(arrived, points, False))
    lat_pairs = [(i, i - 1) for i in range(1, lat_devices)]
    lon_pairs = [(i, (i - 1) % lon_devices) for i in range(lon_devices)]
    both_pairs = [
        (a * lon_devices + c, b * lon_devices + d) for a, b in lat_pairs for c, d in lon_pairs
    ]
    east = lax.ppermute(east, "lon", lon_pairs)
    north = lax.ppermute(north, "lat", lat_pairs)
    corner = lax.ppermute(corner, ("lat", "lon"), both_pairs)
    top = (lax.axis_index("lat") == lat_devices - 1).astype(jnp.int32).reshape(1)
    inside = apply(0, TILES_LAT - 1, (own, east), anomalies, flux_mean)
    return apply(
        TILES_LAT - 1, 1, (top, own, east, north, corner), anomalies, flux_mean, inside
    )


def solution(mesh):
    placed = (
        P(("lat", "lon"), None, None),
        P(("lat", "lon"), None),
        P(("lat", "lon"), None),
        P(("lat", "lon")),
        P(("lat", "lon")),
        P(None, "lat", "lon", None),
        P(None, "lat", "lon"),
    )
    return jax.shard_map(
        shards,
        mesh=mesh,
        in_specs=placed,
        out_specs=(P(None, "lat", "lon", None), P(None, "lat", "lon")),
        check_vma=False,
    )
```

```python
import functools
import math

import jax
import jax.numpy as jnp
from jax import lax
from jax.experimental import pallas as pl
from jax.experimental.pallas import tpu as pltpu
from jax.sharding import PartitionSpec as P

FINE = 25
TILES_LAT = 8
TILES_LON = 8
BLOCK = 16
META = 8
F32 = jnp.float32
BF16 = jnp.bfloat16
NT = (((1,), (1,)), ((), ()))
NN = (((1,), (0,)), ((), ()))


def split(value):
    high = value.astype(BF16)
    return high, (value - high.astype(F32)).astype(BF16)


def dot(left, right, dims=NN):
    return lax.dot_general(left, right, dims, preferred_element_type=F32)


def quotient(value, by):
    if by & (by - 1) == 0:
        return value >> (by.bit_length() - 1), value & (by - 1)
    return lax.div(value, jnp.int32(by)), lax.rem(value, jnp.int32(by))


def place_of(point, columns, lon_devices):
    point_row, point_col = quotient(point, columns)
    device_row, tile_row = quotient(point_row, TILES_LAT)
    device_col, tile_col = quotient(point_col, TILES_LON)
    return device_row * lon_devices + device_col, tile_row * TILES_LON + tile_col


def pack_kernel(columns, lon_devices, capacity, owner, count, pert, prec, dep, *refs):
    outs, (ranks, weights, departs) = refs[:-3], refs[-3:]
    holding, locn, members = pert.shape
    weights[...] = jnp.concatenate([prec[...], prec[...]], axis=1).astype(F32)
    departs[...] = jnp.concatenate([dep[...], dep[...]], axis=1).astype(F32)
    row = lax.broadcasted_iota(jnp.int32, (META, members), 0)
    slot_of_lane = lax.broadcasted_iota(jnp.int32, (META, members), 1) % locn

    def put(out, place, block, within):
        weight = jnp.broadcast_to(weights[pl.ds(block, 1), :], (META, members))
        depart = jnp.broadcast_to(departs[pl.ds(block, 1), :], (META, members))
        out[place, 0:locn, :] = pert[block]
        out[place, locn:, :] = jnp.where(
            row == 0,
            jnp.where(slot_of_lane < count[block], weight, 0.0),
            jnp.where(row == 1, depart, within.astype(F32)),
        ).astype(BF16)

    if len(outs) == 2:
        @pl.loop(0, holding, unroll=4)
        def _(block):
            device, within = place_of(owner[block], columns, lon_devices)
            put(outs[1], device, block, within)
            other = holding - 1 - block
            device, within = place_of(owner[other], columns, lon_devices)
            put(outs[0], device, other, within)

        return

    slots = outs[0].shape[0]

    @pl.loop(0, slots // capacity)
    def _(device):
        ranks[device] = 0

    if slots > holding:

        @pl.loop(0, slots)
        def _(slot):
            outs[0][slot, locn:, :] = jnp.full((META, members), -1, BF16)

    @pl.loop(0, holding)
    def _(block):
        device, within = place_of(owner[block], columns, lon_devices)
        rank = ranks[device]
        ranks[device] = rank + 1
        put(outs[0], device * capacity + jnp.minimum(rank, capacity - 1), block, within)


def pack(owner, count, pert, prec, dep, columns, lon_devices, devices, capacity, halved):
    holding, locn, members = pert.shape
    parts = 2 if halved else 1
    shape = jax.ShapeDtypeStruct((devices * capacity // parts, locn + META, members), BF16)
    vmem = pl.BlockSpec(memory_space=pltpu.VMEM)
    smem = pl.BlockSpec(memory_space=pltpu.SMEM)
    return pl.pallas_call(
        functools.partial(pack_kernel, columns, lon_devices, capacity),
        out_shape=(shape,) * parts,
        in_specs=[smem, smem, vmem, vmem, vmem],
        out_specs=(vmem,) * parts,
        scratch_shapes=[
            pltpu.SMEM((devices,), jnp.int32),
            pltpu.VMEM((holding, members), F32),
            pltpu.VMEM((holding, members), F32),
        ],
        name="pack",
    )(owner, count, pert, prec, dep)


def label_of(meta):
    return jnp.max(meta.astype(F32)[2:3]).astype(jnp.int32)


def load_systems(arrived, systems, rights):
    slots, rows, members = arrived.shape
    locn = rows - META
    points = rights.shape[0]
    lane = lax.broadcasted_iota(jnp.int32, (members + META, members), 1)
    eye = lax.broadcasted_iota(jnp.int32, (members, members), 0) == lax.broadcasted_iota(
        jnp.int32, (members, members), 1
    )
    ridge = jnp.where(eye, members - 1.0, 0.0)

    def one(slot):
        pert = arrived[slot, 0:locn, :]
        meta = arrived[slot, locn:, :].astype(F32)
        weight = meta[0:1]
        depart = meta[1:2]
        twice = jnp.concatenate([pert, pert], axis=0)
        scaled = twice.T.astype(F32) * weight
        line = jnp.broadcast_to(weight * depart, (META, members))
        left = jnp.concatenate([scaled, line], axis=0)
        high = left.astype(BF16).astype(F32)
        both = jnp.where(lane < locn, high, left - high).astype(BF16)
        gram = dot(both, twice)

        def put(place):
            systems[place] = gram[0:members] + ridge
            rights[pl.ds(place, 1), :] = gram[members : members + 1]

        if slots > points:
            label = label_of(arrived[slot, locn:, :])
            pl.when(label >= 0)(lambda: put(label))
        else:
            put(slot)

    def several(step, carry):
        for part in range(8):
            one(step * 8 + part)
        return carry

    lax.fori_loop(0, slots // 8, several, 0)


def diagonal_inverses(step, systems2d, factors, points, members):
    size = BLOCK
    per = members // size
    lane_block = lax.broadcasted_iota(jnp.int32, (points, members), 1) // size
    rows = []
    for half in range(size // per):
        packed = jnp.zeros((points, members), F32)
        for inner in range(per):
            line = systems2d[pl.ds(size * step + per * half + inner, points, stride=members), :]
            line = pltpu.roll(line, (size * (inner - step)) % members, 1)
            packed = jnp.where(lane_block == inner, line, packed)
        turned = packed.T
        for inner in range(per):
            rows.append(turned[size * inner : size * (inner + 1)])
    half = size // 2
    sub = lax.broadcasted_iota(jnp.int32, (half, points), 0)
    rows = [[line[:half], line[half:]] for line in rows]
    spread = lambda line, k: jnp.broadcast_to(
        line[k // half][k % half : k % half + 1], (half, points)
    )
    roots = []
    for k in range(size):
        part = k // half
        root = lax.rsqrt(spread(rows[k], k))
        inverse = root * root
        roots.append(root)
        factors_k = [spread(rows[k], i) for i in range(k + 1, size)]
        line = list(rows[k])
        line[part] = jnp.where(sub == k % half, 1.0, line[part])
        line = [piece * inverse for piece in line]
        for i in range(k + 1, size):
            rows[i][part] = jnp.where(sub == k % half, 0.0, rows[i][part])
            rows[i] = [old - factors_k[i - k - 1] * piece for old, piece in zip(rows[i], line)]
    lower = []
    for i in range(size):
        part = i // half
        line = [piece * roots[i] for piece in rows[i][: part + 1]]
        line[part] = jnp.where(
            sub < i % half, line[part], jnp.where(sub == i % half, roots[i], 0.0)
        )
        lower.append(line)
    nothing = jnp.zeros((half, points), F32)
    whole = []
    for i in range(size):
        total = [nothing, nothing]
        for l in range(i, size):
            factor = spread(lower[l], i)
            for piece in range(l // half + 1):
                term = factor * lower[l][piece]
                total[piece] = term if l == i or (piece and l == half) else total[piece] + term
        whole.append(jnp.concatenate(total, axis=0))
    lower = [jnp.concatenate((line + [nothing])[:2], axis=0) for line in lower]
    for group in range(size // per):
        part = slice(group * per, (group + 1) * per)
        factors[group] = jnp.concatenate(whole[part][::-1], axis=0).T
        factors[size // per + group] = jnp.concatenate(lower[part][::-1], axis=0).T


def solve_kernel(arrived, out, systems2d, rights, factors, slabs):
    points = out.shape[0]
    members = out.shape[2]
    locn = arrived.shape[1] - META
    systems = systems2d.reshape(points, members, members)
    size = BLOCK
    per = members // size
    groups = 2 * size // per
    load_systems(arrived, systems, rights)
    lane8 = lax.broadcasted_iota(jnp.int32, (per, members), 1)
    row = lax.broadcasted_iota(jnp.int32, (members, members), 0) % size
    lane = lax.broadcasted_iota(jnp.int32, (members, members), 1)
    empty = jnp.zeros((members, members), BF16)

    def halves(value):
        high, low = split(value)
        return jnp.concatenate(
            [
                jnp.concatenate([high, low], axis=1),
                jnp.concatenate([high, empty], axis=1),
            ],
            axis=0,
        )

    def product(left, right):
        both = dot(jnp.concatenate(split(left), axis=1), right)
        return both[:, :members] + both[:, members:]

    diagonal_inverses(0, systems2d, factors, points, members)
    for step in range(members // size):
        first = step * size
        after = first + size
        here = (lane >= first) & (lane < after)
        unit = jnp.where(lane - first == row, 1.0, 0.0)

        def small(index):
            start = index * per
            parts = []
            for inner in range(per):
                for group in range(groups):
                    lines = jnp.broadcast_to(
                        factors[group, pl.ds(start + inner, 1), :], (per, members)
                    )
                    move = (size * (inner - per + 1)) % members
                    direct = move if move <= size else 0
                    lines = pltpu.roll(lines, direct, 1, stride=size, stride_axis=0)
                    if move != direct:
                        lines = pltpu.roll(lines, move, 1)
                    parts.append(jnp.where(lane8 // size == inner, lines, 0.0))
            slab = systems[pl.ds(start, per), first:after, :].reshape(members, members)
            right = halves(jnp.where(here, unit, slab))
            both = product(jnp.concatenate(parts, axis=0), right)
            for inner in range(per):
                begin = 2 * size * inner
                slabs[start + inner] = both[begin : begin + size]
                systems[start + inner, first:after, :] = jnp.where(
                    lane[:size] < after, both[begin + size : begin + 2 * size], 0.0
                )

        for index in range(points // per):
            small(index)
        if after == members:
            continue
        def trail(index, begin, stop):
            start = index * per
            rest = stop - begin
            lane_rest = lax.broadcasted_iota(jnp.int32, (rest, members), 1)
            here_rest = (lane_rest >= first) & (lane_rest < after)
            right = halves(slabs[pl.ds(start, per)].reshape(members, members))
            parts = []
            for inner in range(per):
                old = systems[start + inner, begin:stop, :]
                moved = pltpu.roll(old, (size * (inner - step)) % members, 1)
                parts.append(jnp.where(lane_rest // size == inner, moved, 0.0))
            change = product(jnp.concatenate(parts, axis=0), right)
            for inner in range(per):
                old = systems[start + inner, begin:stop, :]
                systems[start + inner, begin:stop, :] = (
                    jnp.where(here_rest, 0.0, old) - change[inner * rest : (inner + 1) * rest]
                )

        for index in range(points // per):
            trail(index, after, after + size)
        diagonal_inverses(step + 1, systems2d, factors, points, members)
        if after + size < members:
            for index in range(points // per):
                trail(index, after + size, members)

    def finish(point):
        inverse = systems[point]
        right = rights[pl.ds(point, 1), :]
        forward = jnp.sum(inverse * right, axis=1, keepdims=True)
        mean = jnp.sum(inverse * forward, axis=0, keepdims=True)
        scaled = (math.sqrt(members - 1.0) * inverse).astype(BF16)
        line = jnp.broadcast_to(mean, (META, members))
        upper = scaled[:half]
        turned = jnp.concatenate([upper, upper], axis=0).T.astype(F32)[:half]
        ready = jnp.where(spare, turned, scaled[half:].astype(F32))
        diagonal = jnp.sum(jnp.where(on_diagonal, upper.astype(F32), 0.0), axis=0, keepdims=True)
        label = arrived[point, locn:, :].astype(F32)
        out[point, 0:half, :] = ready.astype(BF16)
        out[point, half:, :] = jnp.where(
            row8 == 0, line, jnp.where(row8 == 1, diagonal, label)
        ).astype(BF16)

    half = members // 2
    row_half = lax.broadcasted_iota(jnp.int32, (half, members), 0)
    lane_half = lax.broadcasted_iota(jnp.int32, (half, members), 1)
    spare = lane_half - half > row_half
    on_diagonal = lane_half == row_half
    row8 = lax.broadcasted_iota(jnp.int32, (META, members), 0)

    def finish_many(index, carry):
        for part in range(8):
            finish(index * 8 + part)
        return carry

    lax.fori_loop(0, points // 8, finish_many, 0)


def solve(arrived, points):
    slots, rows, members = arrived.shape
    height = members // 2 + META
    vmem = pl.BlockSpec(memory_space=pltpu.VMEM)
    return pl.pallas_call(
        solve_kernel,
        out_shape=jax.ShapeDtypeStruct((points, height, members), BF16),
        in_specs=[vmem],
        out_specs=vmem,
        scratch_shapes=[
            pltpu.VMEM((points * members, members), F32),
            pltpu.VMEM((points, members), F32),
            pltpu.VMEM((2 * BLOCK * BLOCK // members, points, members), F32),
            pltpu.VMEM((points, BLOCK, members), F32),
        ],
        cost_estimate=pl.CostEstimate(
            flops=points * 60_000_000, bytes_accessed=points * 60_000, transcendentals=0
        ),
        name="solve",
    )(arrived)


def merge_kernel(*refs):
    solved, (own, east, north, corner) = refs[:-4], refs[-4:]
    many = 8
    half = own.shape[1] - META

    for array in solved:

        def several(step, carry):
            for part in range(many):
                slot = step * many + part
                place = slot if len(solved) == 1 else label_of(array[slot, half:, :])
                own[place] = array[slot]
            return carry

        lax.fori_loop(0, array.shape[0] // many, several, 0)
    for index in range(TILES_LON):
        north[index] = own[index]
    for index in range(TILES_LAT):
        east[index] = own[index * TILES_LON]
    corner[0] = own[0]


def merge(*arrays):
    shape = lambda count: jax.ShapeDtypeStruct((count,) + arrays[0].shape[1:], BF16)
    vmem = pl.BlockSpec(memory_space=pltpu.VMEM)
    return pl.pallas_call(
        merge_kernel,
        out_shape=(shape(TILES_LAT * TILES_LON), shape(TILES_LAT), shape(TILES_LON), shape(1)),
        in_specs=[vmem] * len(arrays),
        out_specs=(vmem,) * 4,
        name="merge",
    )(*arrays)


def unfolded(folded):
    members = folded.shape[1]
    half = members // 2
    row = lax.broadcasted_iota(jnp.int32, (half, members), 0)
    lane = lax.broadcasted_iota(jnp.int32, (half, members), 1)
    below = lane - half <= row
    lines = folded[:half].astype(F32)
    meta = folded[half:].astype(F32)
    spare = jnp.where(below, 0.0, lines).astype(BF16)
    turned = jnp.concatenate([spare, spare], axis=0).T.astype(F32)[half:]
    upper = jnp.where(
        lane == row,
        jnp.broadcast_to(meta[1:2], (half, members)),
        jnp.where(lane < half, turned, 0.0),
    )
    lower = jnp.where(below, lines, 0.0)
    return jnp.concatenate([upper, lower], axis=0), meta[0:1]


def apply_kernel(first, *refs):
    last = first == TILES_LAT - 1
    if last:
        top, own, east, north, corner, anomalies, flux, _, before, *refs = refs
    else:
        own, east, north, corner, anomalies, flux, *refs = refs
    out, mean, weights, means = refs
    members = anomalies.shape[3]
    cols = anomalies.shape[2]
    step = pl.program_id(1)
    tile_row = step + first
    now = lax.rem(step, 2)
    later = 1 - now
    half = (FINE + 1) // 2
    if last:
        mean[...] = before[...]

    def put(place, col, folded):
        factor, line = unfolded(folded)
        weights[place, col * members : (col + 1) * members, 0:members] = factor.astype(BF16)
        means[place, col : col + 1, :] = line
        return factor

    @pl.when(step == 0)
    def _():
        for col in range(TILES_LON + 1):
            put(now, col, own[col] if col < TILES_LON else east[0])

    for col in range(TILES_LON + 1):
        ahead = north[col] if col < TILES_LON else corner[0]
        if last:
            inner = own[col] if col < TILES_LON else east[0]
            ahead = jnp.where(top[0] == 1, inner, ahead)
        high = put(later, col, ahead)
        place = slice(col * members, (col + 1) * members)
        low = weights[now, place, 0:members].astype(F32)
        change = ((high - low) * (1.0 / FINE)).astype(BF16)
        weights[0, place, members:] = change
        weights[1, place, members:] = change

    width = 32
    offset = lax.broadcasted_iota(jnp.int32, (width, members), 0)
    for part, (start, stop) in enumerate(((0, half), (half, FINE))):
        count = stop - start
        number = jnp.concatenate(
            [jnp.full((1, width, members), line - part * FINE, BF16) for line in range(start, stop)]
        )
        carry = None
        for col in range(TILES_LON):
            begin = col * (FINE - 1)
            field = anomalies[0, start:stop, begin : begin + width, :]
            scaled = field * number
            left = jnp.concatenate([field, scaled], axis=2).reshape(count * width, 2 * members)
            place = slice(col * members, (col + 2) * members)
            both = dot(left, weights[later if part else now, place, :], NT).reshape(count, width, 2 * members)
            cell = offset - col
            inside = (cell >= 0) & (cell < FINE)
            right_weight = jnp.where(inside, cell.astype(F32) / FINE, 0.0)
            left_weight = jnp.where(inside, 1.0 - cell.astype(F32) / FINE, 0.0)
            result = left_weight * both[:, :, :members] + right_weight * both[:, :, members:]
            head = result[:, 0:8]
            if carry is not None:
                head = head + carry
            carry = result[:, width - 8 :]
            out[0, start:stop, begin : begin + width - 8, :] = jnp.concatenate(
                [head, result[:, 8 : width - 8]], axis=1
            ).astype(BF16)
        out[0, start:stop, cols - 8 :, :] = carry.astype(BF16)

    corner_index = lax.broadcasted_iota(jnp.int32, (16, cols), 0)
    cell = lax.broadcasted_iota(jnp.int32, (16, cols), 1)
    tile = cell // FINE
    part = (cell - tile * FINE).astype(F32) / FINE
    hat = jnp.where(
        tile == corner_index, 1.0 - part, jnp.where(tile + 1 == corner_index, part, 0.0)
    )
    keep = lax.broadcasted_iota(jnp.int32, (16, members), 0) <= TILES_LON
    left = jnp.concatenate(
        [jnp.where(keep, means[now], 0.0), jnp.where(keep, means[later], 0.0)], axis=0
    ).astype(BF16)
    for line in range(FINE):
        product = dot(left, anomalies[0, line], NT)
        up = line / FINE
        mixed = (1.0 - up) * product[0:16] + up * product[16:32]
        shift = jnp.sum(mixed * hat, axis=0, keepdims=True)
        place = pl.ds(tile_row * FINE + line, 1)
        mean[0, place, :] = flux[0, place, :] + shift


def apply(first, count, top, own, east, north, corner, anomalies, flux, earlier=()):
    lags, rows, cols, members = anomalies.shape
    height = own.shape[1]
    line = lambda at: pl.BlockSpec((TILES_LON, height, members), lambda l, r: (at(r), 0, 0))
    one = lambda at: pl.BlockSpec((1, height, members), lambda l, r: (at(r), 0, 0))
    strip = pl.BlockSpec((1, FINE, cols, members), lambda l, r: (l, r + first, 0, 0))
    plane = pl.BlockSpec((1, rows, cols), lambda l, r: (l, 0, 0))
    specs = [line(lambda r: r + first), one(lambda r: r + first)]
    operands = [own, east]
    aliases = {}
    if earlier:
        specs = [pl.BlockSpec(memory_space=pltpu.SMEM)] + specs
        specs += [line(lambda r: 0), one(lambda r: 0), strip, plane]
        operands = [top, own, east, north, corner, anomalies, flux]
        aliases = {len(specs): 0, len(specs) + 1: 1}
        specs += [pl.BlockSpec(memory_space=pl.ANY), plane]
        operands += earlier
    else:
        specs += [line(lambda r: r + first + 1), one(lambda r: r + first + 1), strip, plane]
        operands = [own, east, own, east, anomalies, flux]
    cells = count * FINE * cols * lags
    return pl.pallas_call(
        functools.partial(apply_kernel, first),
        grid=(lags, count),
        out_shape=(
            jax.ShapeDtypeStruct(anomalies.shape, BF16),
            jax.ShapeDtypeStruct(flux.shape, F32),
        ),
        in_specs=specs,
        out_specs=(strip, plane),
        scratch_shapes=[
            pltpu.VMEM((2, (TILES_LON + 1) * members, 2 * members), BF16),
            pltpu.VMEM((2, 16, members), F32),
        ],
        input_output_aliases=aliases,
        cost_estimate=pl.CostEstimate(
            flops=cells * members * members * 8,
            bytes_accessed=cells * members * 4,
            transcendentals=0,
        ),
        name="apply_last" if earlier else "apply",
    )(*operands)


def shards(obs_pert, obs_dep, obs_prec, obs_count, owner_point, anomalies, flux_mean):
    lat_devices = lax.axis_size("lat")
    lon_devices = lax.axis_size("lon")
    devices = lat_devices * lon_devices
    holding, locn, members = obs_pert.shape
    capacity = max(1, (holding + devices - 1) // devices)
    columns = TILES_LON * lon_devices
    points = TILES_LAT * TILES_LON
    halved = capacity == 2 and devices * capacity == holding == points
    packed = pack(
        owner_point, obs_count, obs_pert, obs_prec, obs_dep,
        columns, lon_devices, devices, capacity, halved,
    )
    exchange = functools.partial(
        lax.all_to_all, axis_name=("lat", "lon"), split_axis=0, concat_axis=0, tiled=True
    )
    arrived = exchange(packed[0])
    if halved:
        folded = exchange(solve(packed[1], points // 2))
        own, east, north, corner = merge(solve(arrived, points // 2), folded)
    else:
        own, east, north, corner = merge(solve(arrived, points))
    lat_pairs = [(i, i - 1) for i in range(1, lat_devices)]
    lon_pairs = [(i, (i - 1) % lon_devices) for i in range(lon_devices)]
    both_pairs = [
        (a * lon_devices + c, b * lon_devices + d) for a, b in lat_pairs for c, d in lon_pairs
    ]
    east = lax.ppermute(east, "lon", lon_pairs)
    north = lax.ppermute(north, "lat", lat_pairs)
    corner = lax.ppermute(corner, ("lat", "lon"), both_pairs)
    top = (lax.axis_index("lat") == lat_devices - 1).astype(jnp.int32).reshape(1)
    fields = (top, own, east, north, corner, anomalies, flux_mean)
    inside = apply(0, TILES_LAT - 1, *fields)
    return apply(TILES_LAT - 1, 1, *fields, inside)


def solution(mesh):
    placed = (
        P(("lat", "lon"), None, None),
        P(("lat", "lon"), None),
        P(("lat", "lon"), None),
        P(("lat", "lon")),
        P(("lat", "lon")),
        P(None, "lat", "lon", None),
        P(None, "lat", "lon"),
    )
    return jax.shard_map(
        shards,
        mesh=mesh,
        in_specs=placed,
        out_specs=(P(None, "lat", "lon", None), P(None, "lat", "lon")),
        check_vma=False,
    )
```

```python
import functools
import math

import jax
import jax.numpy as jnp
from jax import lax
from jax.experimental import pallas as pl
from jax.experimental.pallas import tpu as pltpu
from jax.sharding import PartitionSpec as P

FINE = 25
TILES_LAT = 8
TILES_LON = 8
BLOCK = 16
META = 8
F32 = jnp.float32
BF16 = jnp.bfloat16
NT = (((1,), (1,)), ((), ()))
NN = (((1,), (0,)), ((), ()))


def split(value):
    high = value.astype(BF16)
    return high, (value - high.astype(F32)).astype(BF16)


def dot(left, right, dims=NN):
    return lax.dot_general(left, right, dims, preferred_element_type=F32)


def quotient(value, by):
    if by & (by - 1) == 0:
        return value >> (by.bit_length() - 1), value & (by - 1)
    return lax.div(value, jnp.int32(by)), lax.rem(value, jnp.int32(by))


def place_of(point, columns, lon_devices):
    point_row, point_col = quotient(point, columns)
    device_row, tile_row = quotient(point_row, TILES_LAT)
    device_col, tile_col = quotient(point_col, TILES_LON)
    return device_row * lon_devices + device_col, tile_row * TILES_LON + tile_col


def pack_kernel(columns, lon_devices, capacity, owner, count, pert, prec, dep, *refs):
    outs, (ranks, weights, departs) = refs[:-3], refs[-3:]
    holding, locn, members = pert.shape
    weights[...] = jnp.concatenate([prec[...], prec[...]], axis=1).astype(F32)
    departs[...] = jnp.concatenate([dep[...], dep[...]], axis=1).astype(F32)
    row = lax.broadcasted_iota(jnp.int32, (META, members), 0)
    slot_of_lane = lax.broadcasted_iota(jnp.int32, (META, members), 1) % locn

    def put(out, place, block, within):
        weight = jnp.broadcast_to(weights[pl.ds(block, 1), :], (META, members))
        depart = jnp.broadcast_to(departs[pl.ds(block, 1), :], (META, members))
        out[place, 0:locn, :] = pert[block]
        out[place, locn:, :] = jnp.where(
            row == 0,
            jnp.where(slot_of_lane < count[block], weight, 0.0),
            jnp.where(row == 1, depart, within.astype(F32)),
        ).astype(BF16)

    if len(outs) == 2:
        @pl.loop(0, holding, unroll=4)
        def _(block):
            device, within = place_of(owner[block], columns, lon_devices)
            put(outs[1], device, block, within)
            other = holding - 1 - block
            device, within = place_of(owner[other], columns, lon_devices)
            put(outs[0], device, other, within)

        return

    slots = outs[0].shape[0]

    @pl.loop(0, slots // capacity)
    def _(device):
        ranks[device] = 0

    if slots > holding:

        @pl.loop(0, slots)
        def _(slot):
            outs[0][slot, locn:, :] = jnp.full((META, members), -1, BF16)

    @pl.loop(0, holding)
    def _(block):
        device, within = place_of(owner[block], columns, lon_devices)
        rank = ranks[device]
        ranks[device] = rank + 1
        put(outs[0], device * capacity + jnp.minimum(rank, capacity - 1), block, within)


def pack(owner, count, pert, prec, dep, columns, lon_devices, devices, capacity, halved):
    holding, locn, members = pert.shape
    parts = 2 if halved else 1
    shape = jax.ShapeDtypeStruct((devices * capacity // parts, locn + META, members), BF16)
    vmem = pl.BlockSpec(memory_space=pltpu.VMEM)
    smem = pl.BlockSpec(memory_space=pltpu.SMEM)
    return pl.pallas_call(
        functools.partial(pack_kernel, columns, lon_devices, capacity),
        out_shape=(shape,) * parts,
        in_specs=[smem, smem, vmem, vmem, vmem],
        out_specs=(vmem,) * parts,
        scratch_shapes=[
            pltpu.SMEM((devices,), jnp.int32),
            pltpu.VMEM((holding, members), F32),
            pltpu.VMEM((holding, members), F32),
        ],
        name="pack",
    )(owner, count, pert, prec, dep)


def label_of(meta):
    return jnp.max(meta.astype(F32)[2:3]).astype(jnp.int32)


def load_systems(arrived, systems, rights):
    slots, rows, members = arrived.shape
    locn = rows - META
    points = rights.shape[0]
    lane = lax.broadcasted_iota(jnp.int32, (members + META, members), 1)
    eye = lax.broadcasted_iota(jnp.int32, (members, members), 0) == lax.broadcasted_iota(
        jnp.int32, (members, members), 1
    )
    ridge = jnp.where(eye, members - 1.0, 0.0)

    def one(slot):
        pert = arrived[slot, 0:locn, :]
        meta = arrived[slot, locn:, :].astype(F32)
        weight = meta[0:1]
        depart = meta[1:2]
        twice = jnp.concatenate([pert, pert], axis=0)
        scaled = twice.T.astype(F32) * weight
        line = jnp.broadcast_to(weight * depart, (META, members))
        left = jnp.concatenate([scaled, line], axis=0)
        high = left.astype(BF16).astype(F32)
        both = jnp.where(lane < locn, high, left - high).astype(BF16)
        gram = dot(both, twice)

        def put(place):
            systems[place] = gram[0:members] + ridge
            rights[pl.ds(place, 1), :] = gram[members : members + 1]

        if slots > points:
            label = label_of(arrived[slot, locn:, :])
            pl.when(label >= 0)(lambda: put(label))
        else:
            put(slot)

    def several(step, carry):
        for part in range(8):
            one(step * 8 + part)
        return carry

    lax.fori_loop(0, slots // 8, several, 0)


def diagonal_inverses(step, systems2d, factors, points, members):
    size = BLOCK
    per = members // size
    lane_block = lax.broadcasted_iota(jnp.int32, (points, members), 1) // size
    rows = []
    for half in range(size // per):
        packed = jnp.zeros((points, members), F32)
        for inner in range(per):
            line = systems2d[pl.ds(size * step + per * half + inner, points, stride=members), :]
            line = pltpu.roll(line, (size * (inner - step)) % members, 1)
            packed = jnp.where(lane_block == inner, line, packed)
        turned = packed.T
        for inner in range(per):
            rows.append(turned[size * inner : size * (inner + 1)])
    half = size // 2
    sub = lax.broadcasted_iota(jnp.int32, (half, points), 0)
    rows = [[line[:half], line[half:]] for line in rows]
    spread = lambda line, k: jnp.broadcast_to(
        line[k // half][k % half : k % half + 1], (half, points)
    )
    roots = []
    for k in range(size):
        part = k // half
        root = lax.rsqrt(spread(rows[k], k))
        inverse = root * root
        roots.append(root)
        factors_k = [spread(rows[k], i) for i in range(k + 1, size)]
        line = list(rows[k])
        line[part] = jnp.where(sub == k % half, 1.0, line[part])
        line = [piece * inverse for piece in line]
        for i in range(k + 1, size):
            rows[i][part] = jnp.where(sub == k % half, 0.0, rows[i][part])
            rows[i] = [old - factors_k[i - k - 1] * piece for old, piece in zip(rows[i], line)]
    lower = []
    for i in range(size):
        part = i // half
        line = [piece * roots[i] for piece in rows[i][: part + 1]]
        line[part] = jnp.where(
            sub < i % half, line[part], jnp.where(sub == i % half, roots[i], 0.0)
        )
        lower.append(line)
    nothing = jnp.zeros((half, points), F32)
    whole = []
    for i in range(size):
        total = [nothing, nothing]
        for l in range(i, size):
            factor = spread(lower[l], i)
            for piece in range(l // half + 1):
                term = factor * lower[l][piece]
                total[piece] = term if l == i or (piece and l == half) else total[piece] + term
        whole.append(jnp.concatenate(total, axis=0))
    lower = [jnp.concatenate((line + [nothing])[:2], axis=0) for line in lower]
    for group in range(size // per):
        part = slice(group * per, (group + 1) * per)
        factors[group] = jnp.concatenate(whole[part][::-1], axis=0).T
        factors[size // per + group] = jnp.concatenate(lower[part][::-1], axis=0).T


def solve_kernel(arrived, out, systems2d, rights, factors, slabs):
    points = out.shape[0]
    members = out.shape[2]
    locn = arrived.shape[1] - META
    systems = systems2d.reshape(points, members, members)
    size = BLOCK
    per = members // size
    groups = 2 * size // per
    load_systems(arrived, systems, rights)
    lane8 = lax.broadcasted_iota(jnp.int32, (per, members), 1)
    row = lax.broadcasted_iota(jnp.int32, (members, members), 0) % size
    lane = lax.broadcasted_iota(jnp.int32, (members, members), 1)
    empty = jnp.zeros((members, members), BF16)

    def halves(value):
        high, low = split(value)
        return jnp.concatenate(
            [
                jnp.concatenate([high, low], axis=1),
                jnp.concatenate([high, empty], axis=1),
            ],
            axis=0,
        )

    def product(left, right):
        both = dot(jnp.concatenate(split(left), axis=1), right)
        return both[:, :members] + both[:, members:]

    diagonal_inverses(0, systems2d, factors, points, members)
    for step in range(members // size):
        first = step * size
        after = first + size
        here = (lane >= first) & (lane < after)
        unit = jnp.where(lane - first == row, 1.0, 0.0)

        def small(index):
            start = index * per
            parts = []
            for inner in range(per):
                for group in range(groups):
                    lines = jnp.broadcast_to(
                        factors[group, pl.ds(start + inner, 1), :], (per, members)
                    )
                    move = (size * (inner - per + 1)) % members
                    direct = move if move <= size else 0
                    lines = pltpu.roll(lines, direct, 1, stride=size, stride_axis=0)
                    if move != direct:
                        lines = pltpu.roll(lines, move, 1)
                    parts.append(jnp.where(lane8 // size == inner, lines, 0.0))
            slab = systems[pl.ds(start, per), first:after, :].reshape(members, members)
            right = halves(jnp.where(here, unit, slab))
            both = product(jnp.concatenate(parts, axis=0), right)
            for inner in range(per):
                begin = 2 * size * inner
                slabs[start + inner] = both[begin : begin + size]
                systems[start + inner, first:after, :] = jnp.where(
                    lane[:size] < after, both[begin + size : begin + 2 * size], 0.0
                )

        for index in range(points // per):
            small(index)
        if after == members:
            continue
        def trail(index, begin, stop):
            start = index * per
            rest = stop - begin
            lane_rest = lax.broadcasted_iota(jnp.int32, (rest, members), 1)
            here_rest = (lane_rest >= first) & (lane_rest < after)
            right = halves(slabs[pl.ds(start, per)].reshape(members, members))
            parts = []
            for inner in range(per):
                old = systems[start + inner, begin:stop, :]
                moved = pltpu.roll(old, (size * (inner - step)) % members, 1)
                parts.append(jnp.where(lane_rest // size == inner, moved, 0.0))
            change = product(jnp.concatenate(parts, axis=0), right)
            for inner in range(per):
                old = systems[start + inner, begin:stop, :]
                systems[start + inner, begin:stop, :] = (
                    jnp.where(here_rest, 0.0, old) - change[inner * rest : (inner + 1) * rest]
                )

        for index in range(points // per):
            trail(index, after, after + size)
        diagonal_inverses(step + 1, systems2d, factors, points, members)
        if after + size < members:
            for index in range(points // per):
                trail(index, after + size, members)

    def finish(point):
        inverse = systems[point]
        right = rights[pl.ds(point, 1), :]
        forward = jnp.sum(inverse * right, axis=1, keepdims=True)
        mean = jnp.sum(inverse * forward, axis=0, keepdims=True)
        scaled = (math.sqrt(members - 1.0) * inverse).astype(BF16)
        line = jnp.broadcast_to(mean, (META, members))
        upper = scaled[:half]
        turned = jnp.concatenate([upper, upper], axis=0).T.astype(F32)[:half]
        ready = jnp.where(spare, turned, scaled[half:].astype(F32))
        diagonal = jnp.sum(jnp.where(on_diagonal, upper.astype(F32), 0.0), axis=0, keepdims=True)
        label = arrived[point, locn:, :].astype(F32)
        out[point, 0:half, :] = ready.astype(BF16)
        out[point, half:, :] = jnp.where(
            row8 == 0, line, jnp.where(row8 == 1, diagonal, label)
        ).astype(BF16)

    half = members // 2
    row_half = lax.broadcasted_iota(jnp.int32, (half, members), 0)
    lane_half = lax.broadcasted_iota(jnp.int32, (half, members), 1)
    spare = lane_half - half > row_half
    on_diagonal = lane_half == row_half
    row8 = lax.broadcasted_iota(jnp.int32, (META, members), 0)

    def finish_many(index, carry):
        for part in range(8):
            finish(index * 8 + part)
        return carry

    lax.fori_loop(0, points // 8, finish_many, 0)


def solve(arrived, points):
    slots, rows, members = arrived.shape
    height = members // 2 + META
    vmem = pl.BlockSpec(memory_space=pltpu.VMEM)
    return pl.pallas_call(
        solve_kernel,
        out_shape=jax.ShapeDtypeStruct((points, height, members), BF16),
        in_specs=[vmem],
        out_specs=vmem,
        scratch_shapes=[
            pltpu.VMEM((points * members, members), F32),
            pltpu.VMEM((points, members), F32),
            pltpu.VMEM((2 * BLOCK * BLOCK // members, points, members), F32),
            pltpu.VMEM((points, BLOCK, members), F32),
        ],
        cost_estimate=pl.CostEstimate(
            flops=points * 60_000_000, bytes_accessed=points * 60_000, transcendentals=0
        ),
        name="solve",
    )(arrived)


def merge_kernel(*refs):
    solved, (own, east, north, corner) = refs[:-4], refs[-4:]
    many = 8
    half = own.shape[1] - META

    for array in solved:

        def several(step, carry):
            for part in range(many):
                slot = step * many + part
                place = slot if len(solved) == 1 else label_of(array[slot, half:, :])
                own[place] = array[slot]
            return carry

        lax.fori_loop(0, array.shape[0] // many, several, 0)
    for index in range(TILES_LON):
        north[index] = own[index]
    for index in range(TILES_LAT):
        east[index] = own[index * TILES_LON]
    corner[0] = own[0]


def merge(*arrays):
    shape = lambda count: jax.ShapeDtypeStruct((count,) + arrays[0].shape[1:], BF16)
    vmem = pl.BlockSpec(memory_space=pltpu.VMEM)
    return pl.pallas_call(
        merge_kernel,
        out_shape=(shape(TILES_LAT * TILES_LON), shape(TILES_LAT), shape(TILES_LON), shape(1)),
        in_specs=[vmem] * len(arrays),
        out_specs=(vmem,) * 4,
        name="merge",
    )(*arrays)


def unfolded(folded):
    members = folded.shape[1]
    half = members // 2
    row = lax.broadcasted_iota(jnp.int32, (half, members), 0)
    lane = lax.broadcasted_iota(jnp.int32, (half, members), 1)
    below = lane - half <= row
    lines = folded[:half].astype(F32)
    meta = folded[half:].astype(F32)
    spare = jnp.where(below, 0.0, lines).astype(BF16)
    turned = jnp.concatenate([spare, spare], axis=0).T.astype(F32)[half:]
    upper = jnp.where(
        lane == row,
        jnp.broadcast_to(meta[1:2], (half, members)),
        jnp.where(lane < half, turned, 0.0),
    )
    lower = jnp.where(below, lines, 0.0)
    return jnp.concatenate([upper, lower], axis=0)


def apply_kernel(
    top, own, east, next_own, next_east, north, corner, anomalies, flux, out, mean, weights
):
    members = anomalies.shape[3]
    cols = anomalies.shape[2]
    step = pl.program_id(1)
    tile_row = step
    now = lax.rem(step, 2)
    later = 1 - now
    from_north = (step == TILES_LAT - 1) & (top[0] == 0)
    half = (FINE + 1) // 2
    def here(col):
        return own[col] if col < TILES_LON else east[0]

    def above(col):
        inner = next_own[col] if col < TILES_LON else next_east[0]
        outer = north[col] if col < TILES_LON else corner[0]
        return jnp.where(from_north, outer, inner)

    def means_of(blocks):
        lines = [block[members // 2 :].astype(F32)[0:1] for block in blocks]
        return jnp.concatenate(lines + [jnp.zeros((16 - len(lines), members), F32)], axis=0)

    columns = range(TILES_LON + 1)
    left = jnp.concatenate(
        [means_of([here(col) for col in columns]), means_of([above(col) for col in columns])],
        axis=0,
    ).astype(BF16)

    def put(place, col, folded):
        factor = unfolded(folded)
        weights[place, col * members : (col + 1) * members, 0:members] = factor.astype(BF16)
        return factor

    @pl.when(step == 0)
    def _():
        for col in columns:
            put(now, col, here(col))

    corner_index = lax.broadcasted_iota(jnp.int32, (16, cols), 0)
    cell = lax.broadcasted_iota(jnp.int32, (16, cols), 1)
    tile = cell // FINE
    part = (cell - tile * FINE).astype(F32) / FINE
    hat = jnp.where(
        tile == corner_index, 1.0 - part, jnp.where(tile + 1 == corner_index, part, 0.0)
    )
    empty = jnp.zeros_like(left)
    double = jnp.concatenate(
        [jnp.concatenate([left, empty], axis=1), jnp.concatenate([empty, left], axis=1)], axis=0
    )
    for begin in range(0, FINE, 2):
        lines = range(begin, min(begin + 2, FINE))
        if len(lines) == 2:
            pair = jnp.concatenate([anomalies[0, line] for line in lines], axis=1)
            product = dot(double, pair, NT)
        else:
            product = dot(left, anomalies[0, begin], NT)
        for line in lines:
            at = (line - begin) * left.shape[0]
            up = line / FINE
            mixed = (1.0 - up) * product[at : at + 16] + up * product[at + 16 : at + 32]
            shift = jnp.sum(mixed * hat, axis=0, keepdims=True)
            place = pl.ds(tile_row * FINE + line, 1)
            mean[0, place, :] = flux[0, place, :] + shift

    for col in columns:
        high = put(later, col, above(col))
        place = slice(col * members, (col + 1) * members)
        low = weights[now, place, 0:members].astype(F32)
        change = ((high - low) * (1.0 / FINE)).astype(BF16)
        weights[0, place, members:] = change
        weights[1, place, members:] = change

    width = 32
    offset = lax.broadcasted_iota(jnp.int32, (width, members), 0)
    for part, (start, stop) in enumerate(((0, half), (half, FINE))):
        count = stop - start
        number = jnp.concatenate(
            [jnp.full((1, width, members), line - part * FINE, BF16) for line in range(start, stop)]
        )
        carry = None
        for col in range(TILES_LON):
            begin = col * (FINE - 1)
            field = anomalies[0, start:stop, begin : begin + width, :]
            scaled = field * number
            left = jnp.concatenate([field, scaled], axis=2).reshape(count * width, 2 * members)
            place = slice(col * members, (col + 2) * members)
            both = dot(left, weights[later if part else now, place, :], NT).reshape(count, width, 2 * members)
            cell = offset - col
            inside = (cell >= 0) & (cell < FINE)
            right_weight = jnp.where(inside, cell.astype(F32) / FINE, 0.0)
            left_weight = jnp.where(inside, 1.0 - cell.astype(F32) / FINE, 0.0)
            result = left_weight * both[:, :, :members] + right_weight * both[:, :, members:]
            head = result[:, 0:8]
            if carry is not None:
                head = head + carry
            carry = result[:, width - 8 :]
            out[0, start:stop, begin : begin + width - 8, :] = jnp.concatenate(
                [head, result[:, 8 : width - 8]], axis=1
            ).astype(BF16)
        out[0, start:stop, cols - 8 :, :] = carry.astype(BF16)


def apply(top, own, east, north, corner, anomalies, flux):
    lags, rows, cols, members = anomalies.shape
    height = own.shape[1]
    line = lambda at: pl.BlockSpec((TILES_LON, height, members), lambda l, r: (at(r), 0, 0))
    one = lambda at: pl.BlockSpec((1, height, members), lambda l, r: (at(r), 0, 0))
    same = lambda r: r
    above = lambda r: jnp.minimum(r + 1, TILES_LAT - 1)
    fixed = lambda r: 0
    strip = pl.BlockSpec((1, FINE, cols, members), lambda l, r: (l, r, 0, 0))
    plane = pl.BlockSpec((1, rows, cols), lambda l, r: (l, 0, 0))
    return pl.pallas_call(
        apply_kernel,
        grid=(lags, TILES_LAT),
        out_shape=(
            jax.ShapeDtypeStruct(anomalies.shape, BF16),
            jax.ShapeDtypeStruct(flux.shape, F32),
        ),
        in_specs=[
            pl.BlockSpec(memory_space=pltpu.SMEM),
            line(same),
            one(same),
            line(above),
            one(above),
            line(fixed),
            one(fixed),
            strip,
            plane,
        ],
        out_specs=(strip, plane),
        scratch_shapes=[
            pltpu.VMEM((2, (TILES_LON + 1) * members, 2 * members), BF16),
        ],
        name="apply",
    )(top, own, east, own, east, north, corner, anomalies, flux)


def shards(obs_pert, obs_dep, obs_prec, obs_count, owner_point, anomalies, flux_mean):
    lat_devices = lax.axis_size("lat")
    lon_devices = lax.axis_size("lon")
    devices = lat_devices * lon_devices
    holding, locn, members = obs_pert.shape
    capacity = max(1, (holding + devices - 1) // devices)
    columns = TILES_LON * lon_devices
    points = TILES_LAT * TILES_LON
    halved = capacity == 2 and devices * capacity == holding == points
    packed = pack(
        owner_point, obs_count, obs_pert, obs_prec, obs_dep,
        columns, lon_devices, devices, capacity, halved,
    )
    exchange = functools.partial(
        lax.all_to_all, axis_name=("lat", "lon"), split_axis=0, concat_axis=0, tiled=True
    )
    arrived = exchange(packed[0])
    if halved:
        folded = exchange(solve(packed[1], points // 2))
        own, east, north, corner = merge(solve(arrived, points // 2), folded)
    else:
        own, east, north, corner = merge(solve(arrived, points))
    lat_pairs = [(i, i - 1) for i in range(1, lat_devices)]
    lon_pairs = [(i, (i - 1) % lon_devices) for i in range(lon_devices)]
    both_pairs = [
        (a * lon_devices + c, b * lon_devices + d) for a, b in lat_pairs for c, d in lon_pairs
    ]
    east = lax.ppermute(east, "lon", lon_pairs)
    north = lax.ppermute(north, "lat", lat_pairs)
    corner = lax.ppermute(corner, ("lat", "lon"), both_pairs)
    top = (lax.axis_index("lat") == lat_devices - 1).astype(jnp.int32).reshape(1)
    return apply(top, own, east, north, corner, anomalies, flux_mean)


def solution(mesh):
    placed = (
        P(("lat", "lon"), None, None),
        P(("lat", "lon"), None),
        P(("lat", "lon"), None),
        P(("lat", "lon")),
        P(("lat", "lon")),
        P(None, "lat", "lon", None),
        P(None, "lat", "lon"),
    )
    return jax.shard_map(
        shards,
        mesh=mesh,
        in_specs=placed,
        out_specs=(P(None, "lat", "lon", None), P(None, "lat", "lon")),
        check_vma=False,
    )
```

```python
import functools
import math

import jax
import jax.numpy as jnp
from jax import lax
from jax.experimental import pallas as pl
from jax.experimental.pallas import tpu as pltpu
from jax.sharding import PartitionSpec as P


FINE = 25
TILES_LAT = 8
TILES_LON = 8
BLOCK = 16
META = 8
F32 = jnp.float32
BF16 = jnp.bfloat16
NT = (((1,), (1,)), ((), ()))
NN = (((1,), (0,)), ((), ()))


def split(value):
    high = value.astype(BF16)
    return high, (value - high.astype(F32)).astype(BF16)


def dot(left, right, dims=NN):
    return lax.dot_general(left, right, dims, preferred_element_type=F32)


def quotient(value, by):
    if by & (by - 1) == 0:
        return value >> (by.bit_length() - 1), value & (by - 1)
    return lax.div(value, jnp.int32(by)), lax.rem(value, jnp.int32(by))


def place_of(point, columns, lon_devices):
    point_row, point_col = quotient(point, columns)
    device_row, tile_row = quotient(point_row, TILES_LAT)
    device_col, tile_col = quotient(point_col, TILES_LON)
    return device_row * lon_devices + device_col, tile_row * TILES_LON + tile_col


def pack_kernel(columns, lon_devices, capacity, owner, count, pert, prec, dep, *refs):
    outs, (ranks, weights, departs) = refs[:-3], refs[-3:]
    holding, locn, members = pert.shape
    weights[...] = jnp.concatenate([prec[...], prec[...]], axis=1).astype(F32)
    departs[...] = jnp.concatenate([dep[...], dep[...]], axis=1).astype(F32)
    row = lax.broadcasted_iota(jnp.int32, (META, members), 0)
    slot_of_lane = lax.broadcasted_iota(jnp.int32, (META, members), 1) % locn

    def put(out, place, block, within):
        weight = jnp.broadcast_to(weights[pl.ds(block, 1), :], (META, members))
        depart = jnp.broadcast_to(departs[pl.ds(block, 1), :], (META, members))
        out[place, 0:locn, :] = pert[block]
        out[place, locn:, :] = jnp.where(
            row == 0,
            jnp.where(slot_of_lane < count[block], weight, 0.0),
            jnp.where(row == 1, depart, within.astype(F32)),
        ).astype(BF16)

    if len(outs) == 2:
        @pl.loop(0, holding, unroll=4)
        def _(block):
            device, within = place_of(owner[block], columns, lon_devices)
            put(outs[1], device, block, within)
            other = holding - 1 - block
            device, within = place_of(owner[other], columns, lon_devices)
            put(outs[0], device, other, within)

        return

    slots = outs[0].shape[0]

    @pl.loop(0, slots // capacity)
    def _(device):
        ranks[device] = 0

    if slots > holding:

        @pl.loop(0, slots)
        def _(slot):
            outs[0][slot, locn:, :] = jnp.full((META, members), -1, BF16)

    @pl.loop(0, holding)
    def _(block):
        device, within = place_of(owner[block], columns, lon_devices)
        rank = ranks[device]
        ranks[device] = rank + 1
        put(outs[0], device * capacity + jnp.minimum(rank, capacity - 1), block, within)


def pack(owner, count, pert, prec, dep, columns, lon_devices, devices, capacity, halved):
    holding, locn, members = pert.shape
    parts = 2 if halved else 1
    shape = jax.ShapeDtypeStruct((devices * capacity // parts, locn + META, members), BF16)
    vmem = pl.BlockSpec(memory_space=pltpu.VMEM)
    smem = pl.BlockSpec(memory_space=pltpu.SMEM)
    return pl.pallas_call(
        functools.partial(pack_kernel, columns, lon_devices, capacity),
        out_shape=(shape,) * parts,
        in_specs=[smem, smem, vmem, vmem, vmem],
        out_specs=(vmem,) * parts,
        scratch_shapes=[
            pltpu.SMEM((devices,), jnp.int32),
            pltpu.VMEM((holding, members), F32),
            pltpu.VMEM((holding, members), F32),
        ],
        name="pack",
    )(owner, count, pert, prec, dep)


def label_of(meta):
    return jnp.max(meta.astype(F32)[2:3]).astype(jnp.int32)


def load_systems(arrived, systems, rights):
    slots, rows, members = arrived.shape
    locn = rows - META
    points = rights.shape[0]
    lane = lax.broadcasted_iota(jnp.int32, (members + META, members), 1)
    eye = lax.broadcasted_iota(jnp.int32, (members, members), 0) == lax.broadcasted_iota(
        jnp.int32, (members, members), 1
    )
    ridge = jnp.where(eye, members - 1.0, 0.0)

    def one(slot):
        pert = arrived[slot, 0:locn, :]
        meta = arrived[slot, locn:, :].astype(F32)
        weight = meta[0:1]
        depart = meta[1:2]
        twice = jnp.concatenate([pert, pert], axis=0)
        scaled = twice.T.astype(F32) * weight
        line = jnp.broadcast_to(weight * depart, (META, members))
        left = jnp.concatenate([scaled, line], axis=0)
        high = left.astype(BF16).astype(F32)
        both = jnp.where(lane < locn, high, left - high).astype(BF16)
        gram = dot(both, twice)

        def put(place):
            systems[place] = gram[0:members] + ridge
            rights[pl.ds(place, 1), :] = gram[members : members + 1]

        if slots > points:
            label = label_of(arrived[slot, locn:, :])
            pl.when(label >= 0)(lambda: put(label))
        else:
            put(slot)

    def several(step, carry):
        for part in range(8):
            one(step * 8 + part)
        return carry

    lax.fori_loop(0, slots // 8, several, 0)


def diagonal_inverses(step, systems2d, factors, points, members):
    size = BLOCK
    per = members // size
    lane_block = lax.broadcasted_iota(jnp.int32, (points, members), 1) // size
    rows = []
    for half in range(size // per):
        packed = jnp.zeros((points, members), F32)
        for inner in range(per):
            line = systems2d[pl.ds(size * step + per * half + inner, points, stride=members), :]
            line = pltpu.roll(line, (size * (inner - step)) % members, 1)
            packed = jnp.where(lane_block == inner, line, packed)
        turned = packed.T
        for inner in range(per):
            rows.append(turned[size * inner : size * (inner + 1)])
    half = size // 2
    sub = lax.broadcasted_iota(jnp.int32, (half, points), 0)
    rows = [[line[:half], line[half:]] for line in rows]
    spread = lambda line, k: jnp.broadcast_to(
        line[k // half][k % half : k % half + 1], (half, points)
    )
    roots = []
    for k in range(size):
        part = k // half
        root = lax.rsqrt(spread(rows[k], k))
        inverse = root * root
        roots.append(root)
        factors_k = [spread(rows[k], i) for i in range(k + 1, size)]
        line = list(rows[k])
        line[part] = jnp.where(sub == k % half, 1.0, line[part])
        line = [piece * inverse for piece in line]
        for i in range(k + 1, size):
            rows[i][part] = jnp.where(sub == k % half, 0.0, rows[i][part])
            rows[i] = [old - factors_k[i - k - 1] * piece for old, piece in zip(rows[i], line)]
    lower = []
    for i in range(size):
        part = i // half
        line = [piece * roots[i] for piece in rows[i][: part + 1]]
        line[part] = jnp.where(
            sub < i % half, line[part], jnp.where(sub == i % half, roots[i], 0.0)
        )
        lower.append(line)
    nothing = jnp.zeros((half, points), F32)
    whole = []
    for i in range(size):
        total = [nothing, nothing]
        for l in range(i, size):
            factor = spread(lower[l], i)
            for piece in range(l // half + 1):
                term = factor * lower[l][piece]
                total[piece] = term if l == i or (piece and l == half) else total[piece] + term
        whole.append(jnp.concatenate(total, axis=0))
    lower = [jnp.concatenate((line + [nothing])[:2], axis=0) for line in lower]
    for group in range(size // per):
        part = slice(group * per, (group + 1) * per)
        factors[group] = jnp.concatenate(whole[part][::-1], axis=0).T
        factors[size // per + group] = jnp.concatenate(lower[part][::-1], axis=0).T


def solve_kernel(arrived, out, systems2d, rights, factors, slabs):
    points = out.shape[0]
    members = out.shape[2]
    locn = arrived.shape[1] - META
    systems = systems2d.reshape(points, members, members)
    size = BLOCK
    per = members // size
    groups = 2 * size // per
    load_systems(arrived, systems, rights)
    lane8 = lax.broadcasted_iota(jnp.int32, (per, members), 1)
    row = lax.broadcasted_iota(jnp.int32, (members, members), 0) % size
    lane = lax.broadcasted_iota(jnp.int32, (members, members), 1)
    empty = jnp.zeros((members, members), BF16)

    def halves(value):
        high, low = split(value)
        return jnp.concatenate(
            [
                jnp.concatenate([high, low], axis=1),
                jnp.concatenate([high, empty], axis=1),
            ],
            axis=0,
        )

    def product(left, right):
        both = dot(jnp.concatenate(split(left), axis=1), right)
        return both[:, :members] + both[:, members:]

    diagonal_inverses(0, systems2d, factors, points, members)
    for step in range(members // size):
        first = step * size
        after = first + size
        here = (lane >= first) & (lane < after)
        unit = jnp.where(lane - first == row, 1.0, 0.0)

        def small(index):
            start = index * per
            parts = []
            for inner in range(per):
                for group in range(groups):
                    lines = jnp.broadcast_to(
                        factors[group, pl.ds(start + inner, 1), :], (per, members)
                    )
                    move = (size * (inner - per + 1)) % members
                    direct = move if move <= size else 0
                    lines = pltpu.roll(lines, direct, 1, stride=size, stride_axis=0)
                    if move != direct:
                        lines = pltpu.roll(lines, move, 1)
                    parts.append(jnp.where(lane8 // size == inner, lines, 0.0))
            slab = systems[pl.ds(start, per), first:after, :].reshape(members, members)
            right = halves(jnp.where(here, unit, slab))
            both = product(jnp.concatenate(parts, axis=0), right)
            for inner in range(per):
                begin = 2 * size * inner
                slabs[start + inner] = both[begin : begin + size]
                systems[start + inner, first:after, :] = jnp.where(
                    lane[:size] < after, both[begin + size : begin + 2 * size], 0.0
                )

        for index in range(points // per):
            small(index)
        if after == members:
            continue

        def trail(index, begin, stop):
            start = index * per
            rest = stop - begin
            lane_rest = lax.broadcasted_iota(jnp.int32, (rest, members), 1)
            here_rest = (lane_rest >= first) & (lane_rest < after)
            right = halves(slabs[pl.ds(start, per)].reshape(members, members))
            parts = []
            for inner in range(per):
                old = systems[start + inner, begin:stop, :]
                moved = pltpu.roll(old, (size * (inner - step)) % members, 1)
                parts.append(jnp.where(lane_rest // size == inner, moved, 0.0))
            change = product(jnp.concatenate(parts, axis=0), right)
            for inner in range(per):
                old = systems[start + inner, begin:stop, :]
                systems[start + inner, begin:stop, :] = (
                    jnp.where(here_rest, 0.0, old) - change[inner * rest : (inner + 1) * rest]
                )

        for index in range(points // per):
            trail(index, after, after + size)
        diagonal_inverses(step + 1, systems2d, factors, points, members)
        if after + size < members:
            for index in range(points // per):
                trail(index, after + size, members)

    def finish(point):
        inverse = systems[point]
        right = rights[pl.ds(point, 1), :]
        forward = jnp.sum(inverse * right, axis=1, keepdims=True)
        mean = jnp.sum(inverse * forward, axis=0, keepdims=True)
        scaled = (math.sqrt(members - 1.0) * inverse).astype(BF16)
        line = jnp.broadcast_to(mean, (META, members))
        upper = scaled[:half]
        turned = jnp.concatenate([upper, upper], axis=0).T.astype(F32)[:half]
        ready = jnp.where(spare, turned, scaled[half:].astype(F32))
        diagonal = jnp.sum(jnp.where(on_diagonal, upper.astype(F32), 0.0), axis=0, keepdims=True)
        label = arrived[point, locn:, :].astype(F32)
        out[point, 0:half, :] = ready.astype(BF16)
        out[point, half:, :] = jnp.where(
            row8 == 0, line, jnp.where(row8 == 1, diagonal, label)
        ).astype(BF16)

    half = members // 2
    row_half = lax.broadcasted_iota(jnp.int32, (half, members), 0)
    lane_half = lax.broadcasted_iota(jnp.int32, (half, members), 1)
    spare = lane_half - half > row_half
    on_diagonal = lane_half == row_half
    row8 = lax.broadcasted_iota(jnp.int32, (META, members), 0)

    def finish_many(index, carry):
        for part in range(8):
            finish(index * 8 + part)
        return carry

    lax.fori_loop(0, points // 8, finish_many, 0)


def solve(arrived, points):
    _, _, members = arrived.shape
    height = members // 2 + META
    vmem = pl.BlockSpec(memory_space=pltpu.VMEM)
    return pl.pallas_call(
        solve_kernel,
        out_shape=jax.ShapeDtypeStruct((points, height, members), BF16),
        in_specs=[vmem],
        out_specs=vmem,
        scratch_shapes=[
            pltpu.VMEM((points * members, members), F32),
            pltpu.VMEM((points, members), F32),
            pltpu.VMEM((2 * BLOCK * BLOCK // members, points, members), F32),
            pltpu.VMEM((points, BLOCK, members), F32),
        ],
        cost_estimate=pl.CostEstimate(
            flops=points * 60_000_000, bytes_accessed=points * 60_000, transcendentals=0
        ),
        name="solve",
    )(arrived)


def merge_kernel(*refs):
    solved, (own, east, north, corner) = refs[:-4], refs[-4:]
    many = 8
    half = own.shape[1] - META

    for array in solved:

        def several(step, carry):
            for part in range(many):
                slot = step * many + part
                place = slot if len(solved) == 1 else label_of(array[slot, half:, :])
                own[place] = array[slot]
            return carry

        lax.fori_loop(0, array.shape[0] // many, several, 0)
    for index in range(TILES_LON):
        north[index] = own[index]
    for index in range(TILES_LAT):
        east[index] = own[index * TILES_LON]
    corner[0] = own[0]


def merge(*arrays):
    shape = lambda count: jax.ShapeDtypeStruct((count,) + arrays[0].shape[1:], BF16)
    vmem = pl.BlockSpec(memory_space=pltpu.VMEM)
    return pl.pallas_call(
        merge_kernel,
        out_shape=(shape(TILES_LAT * TILES_LON), shape(TILES_LAT), shape(TILES_LON), shape(1)),
        in_specs=[vmem] * len(arrays),
        out_specs=(vmem,) * 4,
        name="merge",
    )(*arrays)


def unfolded(folded):
    members = folded.shape[1]
    half = members // 2
    row = lax.broadcasted_iota(jnp.int32, (half, members), 0)
    lane = lax.broadcasted_iota(jnp.int32, (half, members), 1)
    below = lane - half <= row
    lines = folded[:half].astype(F32)
    meta = folded[half:].astype(F32)
    spare = jnp.where(below, 0.0, lines).astype(BF16)
    turned = jnp.concatenate([spare, spare], axis=0).T.astype(F32)[half:]
    upper = jnp.where(
        lane == row,
        jnp.broadcast_to(meta[1:2], (half, members)),
        jnp.where(lane < half, turned, 0.0),
    )
    lower = jnp.where(below, lines, 0.0)
    return jnp.concatenate([upper, lower], axis=0)


def apply_kernel(
    top, own, east, next_own, next_east, far_own, far_east, north, corner, anomalies, flux,
    out, mean, bases, changes, ready_bases, ready_changes,
):
    members = anomalies.shape[3]
    cols = anomalies.shape[2]
    step = pl.program_id(1)
    tile_row = step
    now = lax.rem(step, 2)
    later = 1 - now
    from_north = (step == TILES_LAT - 1) & (top[0] == 0)
    far_north = (step == TILES_LAT - 2) & (top[0] == 0)
    half = (FINE + 1) // 2

    def here(col):
        return own[col] if col < TILES_LON else east[0]

    def above(col):
        inner = next_own[col] if col < TILES_LON else next_east[0]
        outer = north[col] if col < TILES_LON else corner[0]
        return jnp.where(from_north, outer, inner)

    def beyond(col):
        inner = far_own[col] if col < TILES_LON else far_east[0]
        outer = north[col] if col < TILES_LON else corner[0]
        return jnp.where(far_north, outer, inner)

    def means_of(blocks):
        lines = [block[members // 2 :].astype(F32)[0:1] for block in blocks]
        return jnp.concatenate(lines + [jnp.zeros((16 - len(lines), members), F32)], axis=0)

    columns = range(TILES_LON + 1)
    left = jnp.concatenate(
        [means_of([here(col) for col in columns]), means_of([above(col) for col in columns])],
        axis=0,
    ).astype(BF16)

    places = [slice(col * members, (col + 1) * members) for col in columns]

    def prepare(col, folded, slot):
        high = unfolded(folded)
        low = bases[slot, places[col], :].astype(F32)
        ready_bases[places[col], :] = high.astype(BF16)
        ready_changes[places[col], :] = ((high - low) * (1.0 / FINE)).astype(BF16)

    @pl.when(step == 0)
    def _():
        for col in columns:
            bases[now, places[col], :] = unfolded(here(col)).astype(BF16)
            prepare(col, above(col), now)

    bases[later] = ready_bases[...]
    changes[...] = ready_changes[...]

    corner_index = lax.broadcasted_iota(jnp.int32, (16, cols), 0)
    cell = lax.broadcasted_iota(jnp.int32, (16, cols), 1)
    tile = cell // FINE
    part = (cell - tile * FINE).astype(F32) / FINE
    hat = jnp.where(
        tile == corner_index, 1.0 - part, jnp.where(tile + 1 == corner_index, part, 0.0)
    )
    empty = jnp.zeros_like(left)
    double = jnp.concatenate(
        [jnp.concatenate([left, empty], axis=1), jnp.concatenate([empty, left], axis=1)], axis=0
    )
    for begin in range(0, FINE, 2):
        lines = range(begin, min(begin + 2, FINE))
        if len(lines) == 2:
            pair = jnp.concatenate([anomalies[0, line] for line in lines], axis=1)
            product = dot(double, pair, NT)
        else:
            product = dot(left, anomalies[0, begin], NT)
        for line in lines:
            at = (line - begin) * left.shape[0]
            up = line / FINE
            mixed = (1.0 - up) * product[at : at + 16] + up * product[at + 16 : at + 32]
            shift = jnp.sum(mixed * hat, axis=0, keepdims=True)
            place = pl.ds(tile_row * FINE + line, 1)
            mean[0, place, :] = flux[0, place, :] + shift

    width = 32
    offset = lax.broadcasted_iota(jnp.int32, (width, members), 0)
    for part, (start, stop) in enumerate(((0, half), (half, FINE))):
        count = stop - start
        number = jnp.concatenate(
            [jnp.full((1, width, members), line - part * FINE, BF16) for line in range(start, stop)]
        )
        carry = None
        for col in range(TILES_LON):
            begin = col * (FINE - 1)
            field = anomalies[0, start:stop, begin : begin + width, :]
            scaled = field * number
            left = jnp.concatenate([field, scaled], axis=2).reshape(count * width, 2 * members)
            place = slice(col * members, (col + 2) * members)
            right = jnp.concatenate(
                [bases[later if part else now, place, :], changes[place, :]], axis=1
            )
            both = dot(left, right, NT).reshape(count, width, 2 * members)
            cell = offset - col
            inside = (cell >= 0) & (cell < FINE)
            right_weight = jnp.where(inside, cell.astype(F32) / FINE, 0.0)
            left_weight = jnp.where(inside, 1.0 - cell.astype(F32) / FINE, 0.0)
            result = left_weight * both[:, :, :members] + right_weight * both[:, :, members:]
            head = result[:, 0:8]
            if carry is not None:
                head = head + carry
            carry = result[:, width - 8 :]
            out[0, start:stop, begin : begin + width - 8, :] = jnp.concatenate(
                [head, result[:, 8 : width - 8]], axis=1
            ).astype(BF16)
        out[0, start:stop, cols - 8 :, :] = carry.astype(BF16)

    for col in columns:
        prepare(col, beyond(col), later)


def apply(top, own, east, north, corner, anomalies, flux):
    lags, rows, cols, members = anomalies.shape
    height = own.shape[1]
    line = lambda at: pl.BlockSpec((TILES_LON, height, members), lambda l, r: (at(r), 0, 0))
    one = lambda at: pl.BlockSpec((1, height, members), lambda l, r: (at(r), 0, 0))
    same = lambda r: r
    above = lambda r: jnp.minimum(r + 1, TILES_LAT - 1)
    beyond = lambda r: jnp.minimum(r + 2, TILES_LAT - 1)
    fixed = lambda r: 0
    strip = pl.BlockSpec((1, FINE, cols, members), lambda l, r: (l, r, 0, 0))
    plane = pl.BlockSpec((1, rows, cols), lambda l, r: (l, 0, 0))
    return pl.pallas_call(
        apply_kernel,
        grid=(lags, TILES_LAT),
        out_shape=(
            jax.ShapeDtypeStruct(anomalies.shape, BF16),
            jax.ShapeDtypeStruct(flux.shape, F32),
        ),
        in_specs=[
            pl.BlockSpec(memory_space=pltpu.SMEM),
            line(same),
            one(same),
            line(above),
            one(above),
            line(beyond),
            one(beyond),
            line(fixed),
            one(fixed),
            strip,
            plane,
        ],
        out_specs=(strip, plane),
        scratch_shapes=[
            pltpu.VMEM((2, (TILES_LON + 1) * members, members), BF16),
            pltpu.VMEM(((TILES_LON + 1) * members, members), BF16),
            pltpu.VMEM(((TILES_LON + 1) * members, members), BF16),
            pltpu.VMEM(((TILES_LON + 1) * members, members), BF16),
        ],
        name="apply",
    )(top, own, east, own, east, own, east, north, corner, anomalies, flux)


def shards(obs_pert, obs_dep, obs_prec, obs_count, owner_point, anomalies, flux_mean):
    lat_devices = lax.axis_size("lat")
    lon_devices = lax.axis_size("lon")
    devices = lat_devices * lon_devices
    holding, _, _ = obs_pert.shape
    capacity = max(1, (holding + devices - 1) // devices)
    columns = TILES_LON * lon_devices
    points = TILES_LAT * TILES_LON
    halved = capacity == 2 and devices * capacity == holding == points
    packed = pack(
        owner_point, obs_count, obs_pert, obs_prec, obs_dep,
        columns, lon_devices, devices, capacity, halved,
    )
    exchange = functools.partial(
        lax.all_to_all, axis_name=("lat", "lon"), split_axis=0, concat_axis=0, tiled=True
    )
    arrived = exchange(packed[0])
    if halved:
        folded = exchange(solve(packed[1], points // 2))
        own, east, north, corner = merge(solve(arrived, points // 2), folded)
    else:
        own, east, north, corner = merge(solve(arrived, points))
    lat_pairs = [(i, i - 1) for i in range(1, lat_devices)]
    lon_pairs = [(i, (i - 1) % lon_devices) for i in range(lon_devices)]
    both_pairs = [
        (a * lon_devices + c, b * lon_devices + d) for a, b in lat_pairs for c, d in lon_pairs
    ]
    north = lax.ppermute(north, "lat", lat_pairs)
    corner = lax.ppermute(corner, ("lat", "lon"), both_pairs)
    east = lax.ppermute(east, "lon", lon_pairs)
    top = (lax.axis_index("lat") == lat_devices - 1).astype(jnp.int32).reshape(1)
    return apply(top, own, east, north, corner, anomalies, flux_mean)


def solution(mesh):
    placed = (
        P(("lat", "lon"), None, None),
        P(("lat", "lon"), None),
        P(("lat", "lon"), None),
        P(("lat", "lon")),
        P(("lat", "lon")),
        P(None, "lat", "lon", None),
        P(None, "lat", "lon"),
    )
    return jax.shard_map(
        shards,
        mesh=mesh,
        in_specs=placed,
        out_specs=(P(None, "lat", "lon", None), P(None, "lat", "lon")),
        check_vma=False,
    )
```

```python
import functools
import math

import jax
import jax.numpy as jnp
from jax import lax
from jax.experimental import pallas as pl
from jax.experimental.pallas import tpu as pltpu
from jax.sharding import PartitionSpec as P


FINE = 25
TILES_LAT = 8
TILES_LON = 8
BLOCK = 16
META = 8
F32 = jnp.float32
BF16 = jnp.bfloat16
NT = (((1,), (1,)), ((), ()))
NN = (((1,), (0,)), ((), ()))


def split(value):
    high = value.astype(BF16)
    return high, (value - high.astype(F32)).astype(BF16)


def dot(left, right, dims=NN):
    return lax.dot_general(left, right, dims, preferred_element_type=F32)


def quotient(value, by):
    if by & (by - 1) == 0:
        return value >> (by.bit_length() - 1), value & (by - 1)
    return lax.div(value, jnp.int32(by)), lax.rem(value, jnp.int32(by))


def place_of(point, columns, lon_devices):
    point_row, point_col = quotient(point, columns)
    device_row, tile_row = quotient(point_row, TILES_LAT)
    device_col, tile_col = quotient(point_col, TILES_LON)
    return device_row * lon_devices + device_col, tile_row * TILES_LON + tile_col


def pack_kernel(columns, lon_devices, capacity, owner, count, pert, prec, dep, *refs):
    outs, (ranks, weights, departs) = refs[:-3], refs[-3:]
    holding, locn, members = pert.shape
    weights[...] = jnp.concatenate([prec[...], prec[...]], axis=1).astype(F32)
    departs[...] = jnp.concatenate([dep[...], dep[...]], axis=1).astype(F32)
    row = lax.broadcasted_iota(jnp.int32, (META, members), 0)
    slot_of_lane = lax.broadcasted_iota(jnp.int32, (META, members), 1) % locn

    def put(out, place, block, within):
        weight = jnp.broadcast_to(weights[pl.ds(block, 1), :], (META, members))
        depart = jnp.broadcast_to(departs[pl.ds(block, 1), :], (META, members))
        out[place, 0:locn, :] = pert[block]
        out[place, locn:, :] = jnp.where(
            row == 0,
            jnp.where(slot_of_lane < count[block], weight, 0.0),
            jnp.where(row == 1, depart, within.astype(F32)),
        ).astype(BF16)

    if len(outs) == 2:
        @pl.loop(0, holding, unroll=4)
        def _(block):
            device, within = place_of(owner[block], columns, lon_devices)
            put(outs[1], device, block, within)
            other = holding - 1 - block
            device, within = place_of(owner[other], columns, lon_devices)
            put(outs[0], device, other, within)

        return

    slots = outs[0].shape[0]

    @pl.loop(0, slots // capacity)
    def _(device):
        ranks[device] = 0

    if slots > holding:

        @pl.loop(0, slots)
        def _(slot):
            outs[0][slot, locn:, :] = jnp.full((META, members), -1, BF16)

    @pl.loop(0, holding)
    def _(block):
        device, within = place_of(owner[block], columns, lon_devices)
        rank = ranks[device]
        ranks[device] = rank + 1
        put(outs[0], device * capacity + jnp.minimum(rank, capacity - 1), block, within)


def pack(owner, count, pert, prec, dep, columns, lon_devices, devices, capacity, halved):
    holding, locn, members = pert.shape
    parts = 2 if halved else 1
    shape = jax.ShapeDtypeStruct((devices * capacity // parts, locn + META, members), BF16)
    vmem = pl.BlockSpec(memory_space=pltpu.VMEM)
    smem = pl.BlockSpec(memory_space=pltpu.SMEM)
    return pl.pallas_call(
        functools.partial(pack_kernel, columns, lon_devices, capacity),
        out_shape=(shape,) * parts,
        in_specs=[smem, smem, vmem, vmem, vmem],
        out_specs=(vmem,) * parts,
        scratch_shapes=[
            pltpu.SMEM((devices,), jnp.int32),
            pltpu.VMEM((holding, members), F32),
            pltpu.VMEM((holding, members), F32),
        ],
        name="pack",
    )(owner, count, pert, prec, dep)


def label_of(meta):
    return jnp.max(meta.astype(F32)[2:3]).astype(jnp.int32)


def load_systems(arrived, systems, rights):
    slots, rows, members = arrived.shape
    locn = rows - META
    points = rights.shape[0]
    lane = lax.broadcasted_iota(jnp.int32, (members + META, members), 1)
    eye = lax.broadcasted_iota(jnp.int32, (members, members), 0) == lax.broadcasted_iota(
        jnp.int32, (members, members), 1
    )
    ridge = jnp.where(eye, members - 1.0, 0.0)

    def one(slot):
        pert = arrived[slot, 0:locn, :]
        meta = arrived[slot, locn:, :].astype(F32)
        weight = meta[0:1]
        depart = meta[1:2]
        twice = jnp.concatenate([pert, pert], axis=0)
        scaled = twice.T.astype(F32) * weight
        line = jnp.broadcast_to(weight * depart, (META, members))
        left = jnp.concatenate([scaled, line], axis=0)
        high = left.astype(BF16).astype(F32)
        both = jnp.where(lane < locn, high, left - high).astype(BF16)
        gram = dot(both, twice)

        def put(place):
            systems[place] = gram[0:members] + ridge
            rights[pl.ds(place, 1), :] = gram[members : members + 1]

        if slots > points:
            label = label_of(arrived[slot, locn:, :])
            pl.when(label >= 0)(lambda: put(label))
        else:
            put(slot)

    def several(step, carry):
        for part in range(8):
            one(step * 8 + part)
        return carry

    lax.fori_loop(0, slots // 8, several, 0)


def diagonal_inverses(step, systems2d, factors, points, members):
    size = BLOCK
    per = members // size
    lane_block = lax.broadcasted_iota(jnp.int32, (points, members), 1) // size
    rows = []
    for half in range(size // per):
        packed = jnp.zeros((points, members), F32)
        for inner in range(per):
            line = systems2d[pl.ds(size * step + per * half + inner, points, stride=members), :]
            line = pltpu.roll(line, (size * (inner - step)) % members, 1)
            packed = jnp.where(lane_block == inner, line, packed)
        turned = packed.T
        for inner in range(per):
            rows.append(turned[size * inner : size * (inner + 1)])
    half = size // 2
    sub = lax.broadcasted_iota(jnp.int32, (half, points), 0)
    rows = [[line[:half], line[half:]] for line in rows]
    spread = lambda line, k: jnp.broadcast_to(
        line[k // half][k % half : k % half + 1], (half, points)
    )
    roots = []
    for k in range(size):
        part = k // half
        root = lax.rsqrt(spread(rows[k], k))
        inverse = root * root
        roots.append(root)
        factors_k = [spread(rows[k], i) for i in range(k + 1, size)]
        line = list(rows[k])
        line[part] = jnp.where(sub == k % half, 1.0, line[part])
        line = [piece * inverse for piece in line]
        for i in range(k + 1, size):
            rows[i][part] = jnp.where(sub == k % half, 0.0, rows[i][part])
            rows[i] = [old - factors_k[i - k - 1] * piece for old, piece in zip(rows[i], line)]
    lower = []
    for i in range(size):
        part = i // half
        line = [piece * roots[i] for piece in rows[i][: part + 1]]
        line[part] = jnp.where(
            sub < i % half, line[part], jnp.where(sub == i % half, roots[i], 0.0)
        )
        lower.append(line)
    nothing = jnp.zeros((half, points), F32)
    whole = []
    for i in range(size):
        total = [nothing, nothing]
        for l in range(i, size):
            factor = spread(lower[l], i)
            for piece in range(l // half + 1):
                term = factor * lower[l][piece]
                total[piece] = term if l == i or (piece and l == half) else total[piece] + term
        whole.append(jnp.concatenate(total, axis=0))
    lower = [jnp.concatenate((line + [nothing])[:2], axis=0) for line in lower]
    for group in range(size // per):
        part = slice(group * per, (group + 1) * per)
        factors[group] = jnp.concatenate(whole[part][::-1], axis=0).T
        factors[size // per + group] = jnp.concatenate(lower[part][::-1], axis=0).T


def solve_kernel(arrived, out, systems2d, rights, factors, slabs):
    points = out.shape[0]
    members = out.shape[2]
    locn = arrived.shape[1] - META
    systems = systems2d.reshape(points, members, members)
    size = BLOCK
    per = members // size
    groups = 2 * size // per
    load_systems(arrived, systems, rights)
    lane8 = lax.broadcasted_iota(jnp.int32, (per, members), 1)
    row = lax.broadcasted_iota(jnp.int32, (members, members), 0) % size
    lane = lax.broadcasted_iota(jnp.int32, (members, members), 1)
    empty = jnp.zeros((members, members), BF16)

    def halves(value):
        high, low = split(value)
        return jnp.concatenate(
            [
                jnp.concatenate([high, low], axis=1),
                jnp.concatenate([high, empty], axis=1),
            ],
            axis=0,
        )

    def product(left, right):
        both = dot(jnp.concatenate(split(left), axis=1), right)
        return both[:, :members] + both[:, members:]

    diagonal_inverses(0, systems2d, factors, points, members)
    for step in range(members // size):
        first = step * size
        after = first + size
        here = (lane >= first) & (lane < after)
        unit = jnp.where(lane - first == row, 1.0, 0.0)

        def small(index):
            start = index * per
            parts = []
            for inner in range(per):
                for group in range(groups):
                    lines = jnp.broadcast_to(
                        factors[group, pl.ds(start + inner, 1), :], (per, members)
                    )
                    move = (size * (inner - per + 1)) % members
                    direct = move if move <= size else 0
                    lines = pltpu.roll(lines, direct, 1, stride=size, stride_axis=0)
                    if move != direct:
                        lines = pltpu.roll(lines, move, 1)
                    parts.append(jnp.where(lane8 // size == inner, lines, 0.0))
            slab = systems[pl.ds(start, per), first:after, :].reshape(members, members)
            right = halves(jnp.where(here, unit, slab))
            both = product(jnp.concatenate(parts, axis=0), right)
            for inner in range(per):
                begin = 2 * size * inner
                slabs[start + inner] = both[begin : begin + size]
                systems[start + inner, first:after, :] = jnp.where(
                    lane[:size] < after, both[begin + size : begin + 2 * size], 0.0
                )

        for index in range(points // per):
            small(index)
        if after == members:
            continue

        def trail(index, begin, stop):
            start = index * per
            rest = stop - begin
            lane_rest = lax.broadcasted_iota(jnp.int32, (rest, members), 1)
            here_rest = (lane_rest >= first) & (lane_rest < after)
            right = halves(slabs[pl.ds(start, per)].reshape(members, members))
            parts = []
            for inner in range(per):
                old = systems[start + inner, begin:stop, :]
                moved = pltpu.roll(old, (size * (inner - step)) % members, 1)
                parts.append(jnp.where(lane_rest // size == inner, moved, 0.0))
            change = product(jnp.concatenate(parts, axis=0), right)
            for inner in range(per):
                old = systems[start + inner, begin:stop, :]
                systems[start + inner, begin:stop, :] = (
                    jnp.where(here_rest, 0.0, old) - change[inner * rest : (inner + 1) * rest]
                )

        for index in range(points // per):
            trail(index, after, after + size)
        diagonal_inverses(step + 1, systems2d, factors, points, members)
        if after + size < members:
            for index in range(points // per):
                trail(index, after + size, members)

    def finish(point):
        inverse = systems[point]
        right = rights[pl.ds(point, 1), :]
        forward = jnp.sum(inverse * right, axis=1, keepdims=True)
        mean = jnp.sum(inverse * forward, axis=0, keepdims=True)
        scaled = (math.sqrt(members - 1.0) * inverse).astype(BF16)
        line = jnp.broadcast_to(mean, (META, members))
        upper = scaled[:half]
        turned = jnp.concatenate([upper, upper], axis=0).T.astype(F32)[:half]
        ready = jnp.where(spare, turned, scaled[half:].astype(F32))
        diagonal = jnp.sum(jnp.where(on_diagonal, upper.astype(F32), 0.0), axis=0, keepdims=True)
        label = arrived[point, locn:, :].astype(F32)
        out[point, 0:half, :] = ready.astype(BF16)
        out[point, half:, :] = jnp.where(
            row8 == 0, line, jnp.where(row8 == 1, diagonal, label)
        ).astype(BF16)

    half = members // 2
    row_half = lax.broadcasted_iota(jnp.int32, (half, members), 0)
    lane_half = lax.broadcasted_iota(jnp.int32, (half, members), 1)
    spare = lane_half - half > row_half
    on_diagonal = lane_half == row_half
    row8 = lax.broadcasted_iota(jnp.int32, (META, members), 0)

    def finish_many(index, carry):
        for part in range(8):
            finish(index * 8 + part)
        return carry

    lax.fori_loop(0, points // 8, finish_many, 0)


def solve(arrived, points):
    _, _, members = arrived.shape
    height = members // 2 + META
    vmem = pl.BlockSpec(memory_space=pltpu.VMEM)
    return pl.pallas_call(
        solve_kernel,
        out_shape=jax.ShapeDtypeStruct((points, height, members), BF16),
        in_specs=[vmem],
        out_specs=vmem,
        scratch_shapes=[
            pltpu.VMEM((points * members, members), F32),
            pltpu.VMEM((points, members), F32),
            pltpu.VMEM((2 * BLOCK * BLOCK // members, points, members), F32),
            pltpu.VMEM((points, BLOCK, members), F32),
        ],
        cost_estimate=pl.CostEstimate(
            flops=points * 60_000_000, bytes_accessed=points * 60_000, transcendentals=0
        ),
        name="solve",
    )(arrived)


def merge_kernel(*refs):
    solved, (own, east, north, corner) = refs[:-4], refs[-4:]
    many = 8
    half = own.shape[1] - META

    for array in solved:

        def several(step, carry):
            for part in range(many):
                slot = step * many + part
                place = slot if len(solved) == 1 else label_of(array[slot, half:, :])
                own[place] = array[slot]
            return carry

        lax.fori_loop(0, array.shape[0] // many, several, 0)
    for index in range(TILES_LON):
        north[index] = own[index]
    for index in range(TILES_LAT):
        east[index] = own[index * TILES_LON]
    corner[0] = own[0]


def merge(*arrays):
    shape = lambda count: jax.ShapeDtypeStruct((count,) + arrays[0].shape[1:], BF16)
    vmem = pl.BlockSpec(memory_space=pltpu.VMEM)
    return pl.pallas_call(
        merge_kernel,
        out_shape=(shape(TILES_LAT * TILES_LON), shape(TILES_LAT), shape(TILES_LON), shape(1)),
        in_specs=[vmem] * len(arrays),
        out_specs=(vmem,) * 4,
        name="merge",
    )(*arrays)


def unfolded(folded):
    members = folded.shape[1]
    half = members // 2
    row = lax.broadcasted_iota(jnp.int32, (half, members), 0)
    lane = lax.broadcasted_iota(jnp.int32, (half, members), 1)
    below = lane - half <= row
    lines = folded[:half].astype(F32)
    meta = folded[half:].astype(F32)
    spare = jnp.where(below, 0.0, lines).astype(BF16)
    turned = jnp.concatenate([spare, spare], axis=0).T.astype(F32)[half:]
    upper = jnp.where(
        lane == row,
        jnp.broadcast_to(meta[1:2], (half, members)),
        jnp.where(lane < half, turned, 0.0),
    )
    lower = jnp.where(below, lines, 0.0)
    return jnp.concatenate([upper, lower], axis=0)


def apply_kernel(
    top, own, east, next_own, next_east, far_own, far_east, north, corner, anomalies, flux,
    out, mean, bases, changes, ready_bases, ready_changes,
):
    members = anomalies.shape[3]
    cols = anomalies.shape[2]
    step = pl.program_id(1)
    tile_row = step
    now = lax.rem(step, 2)
    later = 1 - now
    from_north = (step == TILES_LAT - 1) & (top[0] == 0)
    far_north = (step == TILES_LAT - 2) & (top[0] == 0)
    half = (FINE + 1) // 2

    def here(col):
        return own[col] if col < TILES_LON else east[0]

    def above(col):
        inner = next_own[col] if col < TILES_LON else next_east[0]
        outer = north[col] if col < TILES_LON else corner[0]
        return jnp.where(from_north, outer, inner)

    def beyond(col):
        inner = far_own[col] if col < TILES_LON else far_east[0]
        outer = north[col] if col < TILES_LON else corner[0]
        return jnp.where(far_north, outer, inner)

    def means_of(blocks):
        lines = [block[members // 2 :].astype(F32)[0:1] for block in blocks]
        return jnp.concatenate(lines + [jnp.zeros((16 - len(lines), members), F32)], axis=0)

    columns = range(TILES_LON + 1)
    left = jnp.concatenate(
        [means_of([here(col) for col in columns]), means_of([above(col) for col in columns])],
        axis=0,
    ).astype(BF16)

    places = [slice(col * members, (col + 1) * members) for col in columns]

    def prepare(col, folded, slot):
        high = unfolded(folded).T
        low = bases[slot, :, places[col]].astype(F32)
        ready_bases[:, places[col]] = high.astype(BF16)
        ready_changes[:, places[col]] = ((high - low) * (1.0 / FINE)).astype(BF16)

    @pl.when(step == 0)
    def _():
        for col in columns:
            bases[now, :, places[col]] = unfolded(here(col)).T.astype(BF16)
            prepare(col, above(col), now)

    bases[later] = ready_bases[...]
    changes[...] = ready_changes[...]

    corner_index = lax.broadcasted_iota(jnp.int32, (16, cols), 0)
    cell = lax.broadcasted_iota(jnp.int32, (16, cols), 1)
    tile = cell // FINE
    part = (cell - tile * FINE).astype(F32) / FINE
    hat = jnp.where(
        tile == corner_index, 1.0 - part, jnp.where(tile + 1 == corner_index, part, 0.0)
    )
    empty = jnp.zeros_like(left)
    double = jnp.concatenate(
        [jnp.concatenate([left, empty], axis=1), jnp.concatenate([empty, left], axis=1)], axis=0
    )
    for begin in range(0, FINE, 2):
        lines = range(begin, min(begin + 2, FINE))
        if len(lines) == 2:
            pair = jnp.concatenate([anomalies[0, line] for line in lines], axis=1)
            product = dot(double, pair, NT)
        else:
            product = dot(left, anomalies[0, begin], NT)
        for line in lines:
            at = (line - begin) * left.shape[0]
            up = line / FINE
            mixed = (1.0 - up) * product[at : at + 16] + up * product[at + 16 : at + 32]
            shift = jnp.sum(mixed * hat, axis=0, keepdims=True)
            place = pl.ds(tile_row * FINE + line, 1)
            mean[0, place, :] = flux[0, place, :] + shift

    width = 32
    offset = lax.broadcasted_iota(jnp.int32, (width, members), 0)
    for part, (start, stop) in enumerate(((0, half), (half, FINE))):
        count = stop - start
        number = jnp.concatenate(
            [jnp.full((1, width, members), line - part * FINE, BF16) for line in range(start, stop)]
        )
        carry = None
        for col in range(TILES_LON):
            begin = col * (FINE - 1)
            field = anomalies[0, start:stop, begin : begin + width, :]
            scaled = field * number
            left = jnp.concatenate([field, scaled], axis=2).reshape(count * width, 2 * members)
            place = slice(col * members, (col + 2) * members)
            right = jnp.concatenate(
                [bases[later if part else now, :, place], changes[:, place]], axis=0
            )
            both = dot(left, right).reshape(count, width, 2 * members)
            cell = offset - col
            inside = (cell >= 0) & (cell < FINE)
            right_weight = jnp.where(inside, cell.astype(F32) / FINE, 0.0)
            left_weight = jnp.where(inside, 1.0 - cell.astype(F32) / FINE, 0.0)
            result = left_weight * both[:, :, :members] + right_weight * both[:, :, members:]
            head = result[:, 0:8]
            if carry is not None:
                head = head + carry
            carry = result[:, width - 8 :]
            out[0, start:stop, begin : begin + width - 8, :] = jnp.concatenate(
                [head, result[:, 8 : width - 8]], axis=1
            ).astype(BF16)
        out[0, start:stop, cols - 8 :, :] = carry.astype(BF16)

    for col in columns:
        prepare(col, beyond(col), later)


def apply(top, own, east, north, corner, anomalies, flux):
    lags, rows, cols, members = anomalies.shape
    height = own.shape[1]
    line = lambda at: pl.BlockSpec((TILES_LON, height, members), lambda l, r: (at(r), 0, 0))
    one = lambda at: pl.BlockSpec((1, height, members), lambda l, r: (at(r), 0, 0))
    same = lambda r: r
    above = lambda r: jnp.minimum(r + 1, TILES_LAT - 1)
    beyond = lambda r: jnp.minimum(r + 2, TILES_LAT - 1)
    fixed = lambda r: 0
    strip = pl.BlockSpec((1, FINE, cols, members), lambda l, r: (l, r, 0, 0))
    plane = pl.BlockSpec((1, rows, cols), lambda l, r: (l, 0, 0))
    return pl.pallas_call(
        apply_kernel,
        grid=(lags, TILES_LAT),
        out_shape=(
            jax.ShapeDtypeStruct(anomalies.shape, BF16),
            jax.ShapeDtypeStruct(flux.shape, F32),
        ),
        in_specs=[
            pl.BlockSpec(memory_space=pltpu.SMEM),
            line(same),
            one(same),
            line(above),
            one(above),
            line(beyond),
            one(beyond),
            line(fixed),
            one(fixed),
            strip,
            plane,
        ],
        out_specs=(strip, plane),
        scratch_shapes=[
            pltpu.VMEM((2, members, (TILES_LON + 1) * members), BF16),
            pltpu.VMEM((members, (TILES_LON + 1) * members), BF16),
            pltpu.VMEM((members, (TILES_LON + 1) * members), BF16),
            pltpu.VMEM((members, (TILES_LON + 1) * members), BF16),
        ],
        name="apply",
    )(top, own, east, own, east, own, east, north, corner, anomalies, flux)


def shards(obs_pert, obs_dep, obs_prec, obs_count, owner_point, anomalies, flux_mean):
    lat_devices = lax.axis_size("lat")
    lon_devices = lax.axis_size("lon")
    devices = lat_devices * lon_devices
    holding, _, _ = obs_pert.shape
    capacity = max(1, (holding + devices - 1) // devices)
    columns = TILES_LON * lon_devices
    points = TILES_LAT * TILES_LON
    halved = capacity == 2 and devices * capacity == holding == points
    packed = pack(
        owner_point, obs_count, obs_pert, obs_prec, obs_dep,
        columns, lon_devices, devices, capacity, halved,
    )
    exchange = functools.partial(
        lax.all_to_all, axis_name=("lat", "lon"), split_axis=0, concat_axis=0, tiled=True
    )
    arrived = exchange(packed[0])
    if halved:
        folded = exchange(solve(packed[1], points // 2))
        own, east, north, corner = merge(solve(arrived, points // 2), folded)
    else:
        own, east, north, corner = merge(solve(arrived, points))
    lat_pairs = [(i, i - 1) for i in range(1, lat_devices)]
    lon_pairs = [(i, (i - 1) % lon_devices) for i in range(lon_devices)]
    both_pairs = [
        (a * lon_devices + c, b * lon_devices + d) for a, b in lat_pairs for c, d in lon_pairs
    ]
    north = lax.ppermute(north, "lat", lat_pairs)
    corner = lax.ppermute(corner, ("lat", "lon"), both_pairs)
    east = lax.ppermute(east, "lon", lon_pairs)
    top = (lax.axis_index("lat") == lat_devices - 1).astype(jnp.int32).reshape(1)
    return apply(top, own, east, north, corner, anomalies, flux_mean)


def solution(mesh):
    placed = (
        P(("lat", "lon"), None, None),
        P(("lat", "lon"), None),
        P(("lat", "lon"), None),
        P(("lat", "lon")),
        P(("lat", "lon")),
        P(None, "lat", "lon", None),
        P(None, "lat", "lon"),
    )
    return jax.shard_map(
        shards,
        mesh=mesh,
        in_specs=placed,
        out_specs=(P(None, "lat", "lon", None), P(None, "lat", "lon")),
        check_vma=False,
    )
```
